256 devices in a mesh: buoy: 4 (over x), dom: 64 (over z, y, core).
Axes of the slice: x: 4, y: 4, z: 8, core: 2. Of those that a mesh axis runs over, the one named last changes fastest.
Arguments:
- ambient: float32 [32, 36, 448], P('buoy', None, 'dom'), may hold values from -6 to 6
- initial_out: float32 [32, 36, 448], P('buoy', None, 'dom'), may hold values from -6 to 6
- translation: bfloat16 [512, 448, 448], P(('buoy', 'dom')), may hold values from -0.0625 to 0.0625
- pair_source: int32 [512], P(('buoy', 'dom')), may hold values from 0 to 31, as said below
- pair_target: int32 [512], P(('buoy', 'dom')), may hold values from 0 to 31, as said below
- pair_live: int32 [512], P(('buoy', 'dom')), may hold values from 0 to 1, as said below
- diffract: bfloat16 [448, 448], P('dom'), may hold values from -0.25 to 0.25
- panel_rows: bfloat16 [8192, 448], P('dom'), may hold values from -0.25 to 0.25
Outputs:
- outgoing: float32 [32, 36, 448], P('buoy', None, 'dom')
- sources: bfloat16 [32, 36, 8192], P('buoy', None, 'dom')
The draws below stay inside these ranges and needn't reach their ends.
Inputs may be any that keep to these rules, and one draw needn't show every extreme that they name: `pair_target`: the slots of one device name target buoys among the 8 buoys of its index of buoy. `pair_source`: A source buoy differs from its target by 1 to 8 places in the farm's order; the live slots of one target name distinct sources. `pair_live`: A slot is live exactly where its source lies inside the farm; some device has all 2 live.
All inputs are finite; a program needn't handle non-finite values.
Results may differ from the reference program's by a relative error of at most 0.015.
Values may be sent and summed in bfloat16 or wider, within the bound.
No kernel may reach another device: no remote copies, remote signals or barrier semaphores. Data moves between devices by JAX's collectives and lax.ppermute only.
A program may use at most 64 MiB of HBM per device.

```python
import jax
import jax.numpy as jnp
from jax import lax

M = 448
H = 36
PANELS = 8192
BD = 8
PD = 2
ITERS = 2
B = 32
PAIRS = 512
N_BUOY = 4
N_DOM = 64


def pair_tables(key):
    base = jax.random.fold_in(key, 11)
    key_order = jax.random.fold_in(base, 5)
    key_slots = jax.random.fold_in(base, 7)
    places = jnp.arange(PAIRS, dtype=jnp.int32)
    group = PAIRS // (B // BD)
    buoy_index = places // group
    slot_keys = jax.random.split(key_slots, B // BD)
    slot_orders = jax.vmap(lambda one_key: jax.random.permutation(one_key, group))(slot_keys).astype(jnp.int32)
    within = slot_orders[buoy_index, places % group]
    target = buoy_index * BD + within % BD
    rank = within // BD
    order_keys = jax.random.split(key_order, B)
    orders = jax.vmap(lambda one_key: jax.random.permutation(one_key, 2 * BD))(order_keys).astype(jnp.int32)
    picked = orders[target, rank]
    delta = jnp.where(picked < BD, picked - BD, picked - BD + 1)
    source = target + delta
    live = ((source >= 0) & (source < B)).astype(jnp.int32)
    source = jnp.clip(source, 0, B - 1)
    return (source.astype(jnp.int32), target.astype(jnp.int32), live)


def draw_pair_source(key, part):
    return pair_tables(key)[0]


def draw_pair_target(key, part):
    return pair_tables(key)[1]


def draw_pair_live(key, part):
    return pair_tables(key)[2]


def levels(own_key, extent, shards, least, high):
    level = 1.0
    for position, parts in shards:
        steps = jax.random.uniform(jax.random.fold_in(jax.random.fold_in(own_key, 6), position), (parts,), jnp.float32, least / len(shards), high / len(shards))
        level = level * jnp.repeat(jnp.exp(steps), extent[position] // parts).reshape((-1,) + (1,) * (len(extent) - 1 - position))
    return level


def scatter_about(own_key, extent, spread, limit, shards=(), held_as=jnp.bfloat16):
    factor_of = levels(own_key, extent, shards, -0.22, 0.18) if shards else 1.0
    result = jax.random.normal(own_key, extent, jnp.float32) * spread * factor_of
    return jnp.minimum(jnp.maximum(result, -limit), limit).astype(held_as)


def setup_inputs(seed: int = 0) -> dict:
    key_of = jax.random.split(jax.random.key(seed), 9)
    return {
        "ambient": scatter_about(key_of[0], (B, H, M), 1.0, 6.0, ((0, 4), (2, 64)), jnp.float32),
        "initial_out": scatter_about(key_of[1], (B, H, M), 1.0, 6.0, ((0, 4), (2, 64)), jnp.float32),
        "translation": scatter_about(key_of[2], (PAIRS, M, M), (M * PD * N_DOM // BD) ** -0.5, 0.0625, ((0, 256),)),
        "pair_source": draw_pair_source(jax.random.fold_in(key_of[8], 71), 0),
        "pair_target": draw_pair_target(jax.random.fold_in(key_of[8], 71), 0),
        "pair_live": draw_pair_live(jax.random.fold_in(key_of[8], 71), 0),
        "diffract": scatter_about(key_of[6], (M, M), M ** -0.5, 0.25, ((0, 64),)),
        "panel_rows": scatter_about(key_of[7], (PANELS, M), M ** -0.5, 0.25, ((0, 64),)),
    }


def rows_product(left, right):
    return lax.dot_general(left, right, (((1,), (1,)), ((), ())), preferred_element_type=jnp.float32)


def reference(ambient, initial_out, translation, pair_source, pair_target, pair_live, diffract, panel_rows):
    group = PD * N_DOM
    blocks = (translation.reshape(N_BUOY, group, M, M),
              pair_source.reshape(N_BUOY, group).astype(jnp.int32),
              pair_target.reshape(N_BUOY, group).astype(jnp.int32),
              pair_live.reshape(N_BUOY, group))
    coeffs = initial_out
    incident_bf = ambient.astype(jnp.bfloat16)
    for step in range(ITERS):
        def add_block(total, block):
            matrices, sources_idx, targets_idx, lives = block
            picked = coeffs[sources_idx].astype(jnp.float32)
            terms = jnp.einsum("phn,pmn->phm", picked, matrices.astype(jnp.float32), precision=lax.Precision.HIGHEST)
            terms = terms * lives.astype(jnp.float32)[:, None, None]
            return total.at[targets_idx].add(terms), None

        incident, unused = lax.scan(add_block, ambient.astype(jnp.float32), blocks)
        incident_bf = incident.astype(jnp.bfloat16)
        coeffs = rows_product(incident_bf.reshape(B * H, M), diffract).reshape(B, H, M)
    sources = rows_product(incident_bf.reshape(B * H, M), panel_rows).astype(jnp.bfloat16).reshape(B, H, PANELS)
    return coeffs, sources
```

```python
import jax
import jax.numpy as jnp
from jax import lax
from jax.sharding import Mesh, PartitionSpec as P

ITERS = 2
Z, Y, C = 8, 4, 2
PLANE = ("z", "y")
F32, BF16 = jnp.float32, jnp.bfloat16


def dot(left, right, left_dim=1, right_dim=0):
    return lax.dot_general(
        left, right, (((left_dim,), (right_dim,)), ((), ())), preferred_element_type=F32
    )


def to_all(block):
    return lax.all_to_all(
        jnp.broadcast_to(block, (Z * Y,) + block.shape), PLANE, 0, 0, tiled=True
    )


def swapped(value):
    return lax.ppermute(value, "c", [(0, 1), (1, 0)])


def with_neighbours(field):
    count = lax.axis_size("x")
    up = [(i, (i + 1) % count) for i in range(count)]
    down = [(b, a) for a, b in up]
    return jnp.concatenate(
        [lax.ppermute(field, "x", up), field, lax.ppermute(field, "x", down)], axis=1
    )


def shards(
    ambient, initial_out, translation, pair_source, pair_target, pair_live, diffract, panel_rows
):
    per_dev, headings, share = initial_out.shape
    full = translation.shape[1]
    half = headings // C
    lanes = half * per_dev
    rows = share * C
    first_buoy = lax.axis_index("x") * per_dev
    core = lax.axis_index("c")

    tables = jnp.stack([pair_source - (first_buoy - per_dev), pair_target - first_buoy, pair_live])
    tables = jnp.concatenate([tables, swapped(tables)], axis=1)
    blocks = (translation, swapped(translation))
    slots = tables.shape[1]

    packed = jnp.concatenate(
        [
            initial_out.transpose(2, 1, 0).reshape(share, headings * per_dev),
            ambient.transpose(2, 1, 0).reshape(share, headings * per_dev),
            diffract.astype(F32),
        ],
        axis=1,
    )
    packed = lax.all_gather(packed, "c", axis=0, tiled=True)
    first = lax.dynamic_slice_in_dim(packed, core * lanes, lanes, 1).astype(BF16)
    own_ambient = lax.dynamic_slice_in_dim(packed, C * lanes + core * lanes, lanes, 1)
    message = jnp.concatenate([first, packed[:, 2 * C * lanes :].astype(BF16)], axis=1)
    everything = to_all(message).reshape(full, -1)
    coeffs = everything[:, :lanes]
    matrix = everything[:, lanes:]

    src = lax.broadcasted_iota(jnp.int32, (3, half, per_dev, slots, half, per_dev), 0) * per_dev
    src = src + lax.broadcasted_iota(jnp.int32, src.shape, 2)
    same = lax.broadcasted_iota(jnp.int32, src.shape, 1) == lax.broadcasted_iota(
        jnp.int32, src.shape, 4
    )
    tgt = lax.broadcasted_iota(jnp.int32, src.shape, 5)
    table = lambda i: tables[i][None, None, None, :, None, None]
    select = (same & (src == table(0)) & (tgt == table(1)) & (table(2) == 1)).astype(BF16)
    select = select.reshape(3 * lanes, slots * lanes)

    incident = None
    for step in range(ITERS):
        if step:
            coeffs = dot(matrix, incident).astype(BF16)
        picked = dot(with_neighbours(coeffs), select).astype(BF16)
        total = 0
        for i in range(slots):
            block = blocks[i // 2][i % 2]
            total = total + dot(block, picked[:, i * lanes : (i + 1) * lanes])
        parts = lax.all_to_all(
            total.astype(BF16).reshape(Z * Y, rows, lanes), PLANE, 0, 0, tiled=True
        )
        own = own_ambient + jnp.sum(parts.astype(F32), axis=0)
        incident = to_all(own.astype(BF16)).reshape(full, lanes)

    whole = lax.all_gather(incident, "c", axis=0, tiled=False)
    sources = lax.dot_general(
        whole, panel_rows, (((1,), (1,)), ((), ())), preferred_element_type=F32
    ).astype(BF16)
    sources = sources.reshape(headings, per_dev, panel_rows.shape[0]).transpose(1, 0, 2)
    outgoing = lax.dot_general(
        diffract, whole, (((1,), (1,)), ((), ())), preferred_element_type=F32
    )
    outgoing = outgoing.reshape(share, headings, per_dev).transpose(2, 1, 0)
    return outgoing, sources


def solution(mesh):
    fine = Mesh(mesh.devices.reshape(mesh.shape["buoy"], Z, Y, C), ("x", "z", "y", "c"))
    dom = ("z", "y", "c")
    in_specs = (
        P("x", None, dom),
        P("x", None, dom),
        P(("x",) + dom, None, None),
        P(("x",) + dom),
        P(("x",) + dom),
        P(("x",) + dom),
        P(dom, None),
        P(dom, None),
    )
    out_specs = (P("x", None, dom), P("x", None, dom))
    return jax.shard_map(shards, mesh=fine, in_specs=in_specs, out_specs=out_specs, check_vma=False)
```

```python
import functools

import jax
import jax.numpy as jnp
from jax import lax
from jax.experimental import pallas as pl
from jax.experimental.pallas import tpu as pltpu
from jax.sharding import Mesh, PartitionSpec as P

ITERS = 2
Z, Y, C = 8, 4, 2
PLANE = ("z", "y")
CHIPS = Z * Y
F32, BF16, I32 = jnp.float32, jnp.bfloat16, jnp.int32

BD, H, S, M = 8, 36, 7, 448
HC, R, BLK, L = H // C, S * C, 16, 256
LAN = HC * BD
ROWS = CHIPS * BLK
HALF = M // C
SOURCES = 3 * BD
EMPTY = SOURCES * BD


def iota(shape, dim):
    return lax.broadcasted_iota(I32, shape, dim)


def ones(cond):
    return jnp.where(cond, 1.0, 0.0).astype(BF16)


def dot(left, right, dims=(1, 0), exact=False):
    return lax.dot_general(
        left,
        right,
        (((dims[0],), (dims[1],)), ((), ())),
        preferred_element_type=F32,
        precision=lax.Precision.HIGHEST if exact else None,
    )


def shift(rows, cols, start, to, width):
    row, col = iota((rows, cols), 0), iota((rows, cols), 1)
    return ones((row - start == col - to) & (col >= to) & (col < to + width))


def padding():
    row, col = iota((ROWS, M), 0), iota((ROWS, M), 1)
    return ones((col == row - 2 * (row >> 4)) & ((row & 15) < R))


def packing():
    row, col = iota((M, ROWS), 0), iota((M, ROWS), 1)
    return ones((row == col - 2 * (col >> 4)) & ((col & 15) < R))


def chip_field(own, other, core, exact):
    kind = F32 if exact else BF16
    head, lane = iota((H, L), 0), iota((H, L), 1)
    spread = ones((head == core * HC + (lane >> 3)) & (lane < LAN)).astype(kind)
    row, lane = iota((S * BD, L), 0), iota((S * BD, L), 1)
    total = 0.0
    for value, place in ((own, core), (other, 1 - core)):
        wide = dot(value.reshape(S * BD, H).astype(kind), spread, exact=exact)
        wide = jnp.where((row & 7) == (lane & 7), wide, 0.0)
        to, col = iota((BLK, S * BD), 0), iota((BLK, S * BD), 1)
        gather = ones((col >> 3) == to - S * place).astype(kind)
        total = total + dot(gather, wide.astype(kind), exact=exact)
    return total


def send_kernel(scalars, own_ref, other_ref, t_ref, out_ref):
    field = chip_field(own_ref[...], other_ref[...], scalars[0], False)
    row, lane = iota((BLK, 128), 0), iota((BLK, 128), 1)
    frow, fcol = iota((L, 128), 0), iota((L, 128), 1)
    tail = dot(field.astype(BF16), ones(frow == 128 + (fcol & 15)))
    tail = jnp.where((lane >> 4) == (row & 7), tail, 0.0)
    to, col = iota((BLK, BLK), 0), iota((BLK, BLK), 1)
    tail = dot(ones((to == R + (col >> 3)) & (col < R)), tail.astype(BF16))
    block = jnp.where(row < R, field[:, :128], tail)
    corner = (
        dot(block.astype(BF16), shift(128, 128, 0, 64, 64)),
        jnp.where(lane >= 64, block, 0.0),
    )
    pad = padding()
    widen = shift(64, 128, 0, 0, 64)
    for p in range(2):
        number = jnp.where((row == BLK - 1) & (lane == 0), scalars[1 + p].astype(F32), 0.0)
        for q in range(3):
            part = dot(pad, t_ref[p, :, 128 * q : 128 * (q + 1)]).reshape(CHIPS, BLK, 128)
            if q == 0:
                part = part + number[None]
            at = 512 * p + 128 * q
            out_ref[:, :, at : at + 128] = part.astype(BF16)
        last = dot(t_ref[p, :, 384:M], widen).astype(BF16)
        part = dot(pad, last).reshape(CHIPS, BLK, 128) + corner[p][None]
        out_ref[:, :, 512 * p + 384 : 512 * p + 512] = part.astype(BF16)


def first_kernel(in_ref, out_ref):
    third = in_ref[:, :, 384:512].reshape(ROWS, 128)
    last = in_ref[:, :, 896:1024].reshape(ROWS, 128)
    row, lane = iota((ROWS, 128), 0), iota((ROWS, 128), 1)
    block = dot(third, shift(128, 128, 64, 0, 64)) + jnp.where(lane >= 64, last.astype(F32), 0.0)
    block = block.astype(BF16)
    to, col = iota((ROWS, ROWS), 0), iota((ROWS, ROWS), 1)
    tail = dot(ones(col == (to - (to & 15)) + R + ((to & 15) >> 3)), block)
    tail = jnp.where((lane >> 4) == (row & 7), tail, 0.0).astype(BF16)
    frow, fcol = iota((128, 128), 0), iota((128, 128), 1)
    tail = dot(tail, ones((fcol == (frow & 15)) & (fcol < 16))).astype(BF16)
    pack = packing()
    out_ref[:, :128] = dot(pack, block).astype(BF16)
    out_ref[:, 128:] = dot(pack, tail).astype(BF16)


def place_kernel(
    scalars, own_at, other_at, in_ref, other_ref, amb_ref, amb_other_ref, d_ref, w_ref, a_ref, dm_ref
):
    w_ref[...] = jnp.zeros_like(w_ref)
    for j in range(CHIPS):
        for p in range(2):
            w_ref[own_at[j, p]] = in_ref[j, :, 512 * p : 512 * (p + 1)]
            w_ref[other_at[j, p]] = other_ref[j, :, 512 * p : 512 * (p + 1)]
    a_ref[...] = chip_field(amb_ref[...], amb_other_ref[...], scalars[0], True)
    to, col = iota((BLK, S), 0), iota((BLK, S), 1)
    matrix = d_ref[...].astype(F32)
    halves = 0.0
    for k in range(2):
        half = dot(ones(to == col + S * k).astype(F32), matrix, exact=True)
        halves = halves + dot(half.astype(BF16), shift(M, L, HALF * k, 0, HALF))
    halves = halves.astype(BF16)
    dm_ref[:, :128] = dot(halves, shift(L, 128, 128, 32, HALF - 128)).astype(BF16)
    dm_ref[:, 128:] = halves[:, :128]


def incident_kernel(w_ref, low_ref, own_ref, high_ref, a_ref, *rest):
    out_ref = rest[-1]
    lane = iota((BD * BLK, L), 1)
    total = jnp.zeros((BD * BLK, L), F32)
    for g, field in enumerate((low_ref, own_ref, high_ref)):
        for b in range(BD):
            part = dot(w_ref[BD * g + b, :, :M], field[...])
            total = total + jnp.where((lane & 7) == b, part, 0.0)
    row, col = iota((L, L), 0), iota((L, L), 1)
    same = ones(((row >> 3) == (col >> 3)) & (row < LAN)).astype(F32)
    total = dot(total, same, exact=True)
    row, lane = iota((BLK, L), 0), iota((BLK, L), 1)
    mine = a_ref[...]
    for t in range(BD):
        mine = mine + jnp.where((lane & 7) == t, total[BLK * t : BLK * (t + 1)], 0.0)
    mine = jnp.where((row < R) & (lane < LAN), mine, 0.0)
    first, second = mine[:, :128], mine[:, 128:]
    if len(rest) == 2:
        second = second + rest[0][:, :128].astype(F32)
        third = rest[0][:, 128:]
        out_ref[:, :, 256:] = jnp.broadcast_to(third[None], (CHIPS, BLK, 128))
    out_ref[:, :, :128] = jnp.broadcast_to(first.astype(BF16)[None], (CHIPS, BLK, 128))
    out_ref[:, :, 128:256] = jnp.broadcast_to(second.astype(BF16)[None], (CHIPS, BLK, 128))


def coeffs_kernel(scalars, in_ref, other_ref, out_ref):
    core = scalars[0]
    lane = iota((ROWS, L), 1)
    field = jnp.where(lane < LAN, in_ref[:, :, :L].reshape(ROWS, L).astype(F32), 0.0).astype(BF16)
    field = dot(packing(), field).astype(BF16)
    back = shift(128, 128, 32, 0, HALF - 128)
    row, col = iota((M, ROWS), 0), iota((M, ROWS), 1)
    first = 14 * (col >> 4) + (col & 15)
    left, right = [0.0, 0.0], [0.0, 0.0]
    for ref, place in ((in_ref, core), (other_ref, 1 - core)):
        low = ref[:, :, 256:384].reshape(ROWS, 128)
        high = dot(ref[:, :, 128:256].reshape(ROWS, 128), back).astype(BF16)
        above = ones((row == first + S * place) & ((col & 15) < S))
        below = ones((row == first - S + S * place) & ((col & 15) >= S) & ((col & 15) < R))
        for i, part in enumerate((low, high)):
            left[i] = left[i] + dot(above, part)
            right[i] = right[i] + dot(below, part)
    rest = HALF - 128
    total = dot(left[0].astype(BF16), field[:128])
    total = total + dot(left[1].astype(BF16)[:, :rest], field[128:HALF])
    total = total + dot(right[0].astype(BF16), field[HALF : HALF + 128])
    total = total + dot(right[1].astype(BF16)[:, :rest], field[HALF + 128 :])
    out_ref[...] = total.astype(BF16)


def last_kernel(in_ref, p_ref, d_ref, src_ref, out_ref):
    panels = dot(padding(), p_ref[...]).astype(BF16)
    matrix = dot(d_ref[...], packing()).astype(BF16)
    out = 0.0
    for c in range(C):
        field = in_ref[c].reshape(ROWS, L)
        part = dot(field, panels, dims=(0, 0))
        src_ref[LAN * c : LAN * (c + 1), :] = part[:LAN].astype(BF16)
        row, col = iota((L, BD * 128), 0), iota((L, BD * 128), 1)
        to = (row & 7) * 128 + (row >> 3) + HC * c
        wide = dot(field, ones((col == to) & (row < LAN))).astype(BF16)
        out = out + dot(matrix, wide)
    for b in range(BD):
        out_ref[:, b, :] = out[:, 128 * b : 128 * b + H]


VM = pl.BlockSpec(memory_space=pltpu.VMEM)
SM = pl.BlockSpec(memory_space=pltpu.SMEM)


def call(kernel, scalars, arrays, shapes, name):
    return pl.pallas_call(
        kernel,
        out_shape=shapes,
        in_specs=[SM] * len(scalars) + [VM] * len(arrays),
        out_specs=[VM] * len(shapes) if isinstance(shapes, tuple) else VM,
        compiler_params=pltpu.CompilerParams(vmem_limit_bytes=40 << 20),
        name=name,
    )(*scalars, *arrays)


def shape(*dims, dtype=BF16):
    return jax.ShapeDtypeStruct(dims, dtype)


def exchange(blocks):
    return lax.all_to_all(blocks, PLANE, 0, 0, tiled=True)


def swapped(value):
    return lax.ppermute(value, "c", [(0, 1), (1, 0)])


def with_neighbours(field):
    count = lax.axis_size("x")
    up = [(i, (i + 1) % count) for i in range(count)]
    down = [(b, a) for a, b in up]
    return lax.ppermute(field, "x", up), field, lax.ppermute(field, "x", down)


def slot_numbers(blocks):
    return jnp.stack([blocks[:, BLK - 1, 0], blocks[:, BLK - 1, 512]], axis=1).astype(I32)


def shards(
    ambient, initial_out, translation, pair_source, pair_target, pair_live, diffract, panel_rows
):
    first_buoy = lax.axis_index("x") * BD
    core = lax.axis_index("c")
    at = (pair_source - first_buoy + BD) * BD + pair_target - first_buoy
    at = jnp.where(pair_live == 1, jnp.clip(at, 0, EMPTY), EMPTY)
    scalars = jnp.concatenate([core[None], at]).astype(I32)

    begin = initial_out.transpose(2, 0, 1)
    waves = ambient.transpose(2, 0, 1)
    message = call(
        send_kernel,
        (scalars,),
        (begin, swapped(begin), translation),
        shape(CHIPS, BLK, 1024),
        "send",
    )
    got = exchange(message)
    got, waves, diffract, panel_rows = lax.optimization_barrier((got, waves, diffract, panel_rows))
    coeffs = call(first_kernel, (), (got,), shape(M, L), "first")
    around = with_neighbours(coeffs)
    got_other = swapped(got)
    matrices, own_waves, rows = call(
        place_kernel,
        (scalars, slot_numbers(got), slot_numbers(got_other)),
        (got, got_other, waves, swapped(waves), diffract),
        (shape(EMPTY + BD, BLK, 512), shape(BLK, L, dtype=F32), shape(BLK, L)),
        "place",
    )
    matrices = matrices.reshape(SOURCES + 1, BD * BLK, 512)

    message = call(
        incident_kernel,
        (),
        (matrices, *around, own_waves, rows),
        shape(CHIPS, BLK, 384),
        "incident_first",
    )
    got = exchange(message)
    coeffs = call(coeffs_kernel, (scalars,), (got, swapped(got)), shape(M, L), "coeffs")
    message = call(
        incident_kernel,
        (),
        (matrices, *with_neighbours(coeffs), own_waves),
        shape(CHIPS, BLK, L),
        "incident_last",
    )
    whole = lax.all_gather(exchange(message), "c", axis=0, tiled=False)
    sources, outgoing = call(
        last_kernel,
        (),
        (whole, panel_rows.T, diffract),
        (shape(H * BD, panel_rows.shape[0]), shape(S, BD, H, dtype=F32)),
        "last",
    )
    sources = sources.reshape(H, BD, panel_rows.shape[0]).transpose(1, 0, 2)
    return outgoing.transpose(1, 2, 0), sources


def solution(mesh):
    fine = Mesh(mesh.devices.reshape(mesh.shape["buoy"], Z, Y, C), ("x", "z", "y", "c"))
    dom = ("z", "y", "c")
    in_specs = (
        P("x", None, dom),
        P("x", None, dom),
        P(("x",) + dom, None, None),
        P(("x",) + dom),
        P(("x",) + dom),
        P(("x",) + dom),
        P(dom, None),
        P(dom, None),
    )
    out_specs = (P("x", None, dom), P("x", None, dom))
    return jax.shard_map(shards, mesh=fine, in_specs=in_specs, out_specs=out_specs, check_vma=False)
```

```python
import jax
import jax.numpy as jnp
from jax import lax
from jax.experimental import pallas as pl
from jax.experimental.pallas import tpu as pltpu
from jax.sharding import Mesh, PartitionSpec as P

ITERS = 2
Z, Y, C = 8, 4, 2
PLANE = ("z", "y")
CHIPS = Z * Y
F32, BF16, I32 = jnp.float32, jnp.bfloat16, jnp.int32

BD, H, S, M = 8, 36, 7, 448
HC, R, BLK, L = H // C, S * C, 16, 256
LAN = HC * BD
ROWS = CHIPS * BLK
HALF = M // C
SOURCES = 3 * BD
EMPTY = SOURCES * BD


def iota(shape, dim):
    return lax.broadcasted_iota(I32, shape, dim)


def ones(cond):
    return jnp.where(cond, 1.0, 0.0).astype(BF16)


def dot(left, right, dims=(1, 0), exact=False):
    return lax.dot_general(
        left,
        right,
        (((dims[0],), (dims[1],)), ((), ())),
        preferred_element_type=F32,
        precision=lax.Precision.HIGHEST if exact else None,
    )


def shift(rows, cols, start, to, width):
    row, col = iota((rows, cols), 0), iota((rows, cols), 1)
    return ones((row - start == col - to) & (col >= to) & (col < to + width))


def padding():
    row, col = iota((ROWS, M), 0), iota((ROWS, M), 1)
    return ones((col == row - 2 * (row >> 4)) & ((row & 15) < R))


def packing():
    row, col = iota((M, ROWS), 0), iota((M, ROWS), 1)
    return ones((row == col - 2 * (col >> 4)) & ((col & 15) < R))


def packed(field):
    rows = field.shape[0]
    frow, fcol = iota((128, 128), 0), iota((128, 128), 1)
    tail = dot(field[:, 128:].astype(BF16), ones(frow == (fcol & 15)))
    row, lane = iota((rows, 128), 0), iota((rows, 128), 1)
    tail = jnp.where(((lane >> 4) == (row & 7)) & ((row & 15) < R), tail, 0.0).astype(BF16)
    to, col = iota((rows, rows), 0), iota((rows, rows), 1)
    same = (to >> 4) == (col >> 4)
    tail = dot(ones(same & ((to & 15) == R + ((col & 15) >> 3)) & ((col & 15) < R)), tail)
    return jnp.where((row & 15) < R, field[:, :128], tail).astype(BF16)


def unpacked(blocks):
    row, lane = iota((M, 128), 0), iota((M, 128), 1)
    place = row - R * ((row * 4682) >> 16)
    to, col = iota((M, ROWS), 0), iota((M, ROWS), 1)
    chip = (to * 4682) >> 16
    spare = ones(col == BLK * chip + R + ((to - R * chip) >> 3))
    tail = jnp.where((lane >> 4) == (place & 7), dot(spare, blocks), 0.0).astype(BF16)
    frow, fcol = iota((128, 128), 0), iota((128, 128), 1)
    tail = dot(tail, ones((fcol == (frow & 15)) & (fcol < 16)))
    return jnp.concatenate([dot(packing(), blocks), tail], axis=1).astype(BF16)


def chip_field(own, other, core, exact):
    kind = F32 if exact else BF16
    head, lane = iota((H, L), 0), iota((H, L), 1)
    spread = ones((head == core * HC + (lane >> 3)) & (lane < LAN)).astype(kind)
    row, lane = iota((S * BD, L), 0), iota((S * BD, L), 1)
    total = 0.0
    for value, place in ((own, core), (other, 1 - core)):
        wide = dot(value.reshape(S * BD, H).astype(kind), spread, exact=exact)
        wide = jnp.where((row & 7) == (lane & 7), wide, 0.0)
        to, col = iota((BLK, S * BD), 0), iota((BLK, S * BD), 1)
        gather = ones((col >> 3) == to - S * place).astype(kind)
        total = total + dot(gather, wide.astype(kind), exact=exact)
    return total


def send_kernel(where_am_i, source, target, live, t_hbm, d_hbm, out_ref, t_ref, d_ref, sems):
    copies = [pltpu.make_async_copy(d_hbm, d_ref, sems.at[0])]
    copies += [pltpu.make_async_copy(t_hbm.at[p], t_ref.at[p], sems.at[1 + p]) for p in range(2)]
    for copy in copies:
        copy.start()
    buoy = where_am_i[1]
    pad = padding()
    widen = shift(64, 128, 0, 0, 64)
    row, col = iota((M, M), 0), iota((M, M), 1)
    row = row - HALF * (buoy & 1)
    twice = ones((row == jnp.where(col < HALF, col, col - HALF)))
    to, slot_row = iota((BLK, S), 0), iota((BLK, S), 1)
    lane = iota((S, M), 1)
    brow, blane = iota((BLK, 128), 0), iota((BLK, 128), 1)
    copies[0].wait()
    both = dot(d_ref[...], twice)
    low = jnp.where(lane < HALF, both, 0.0).astype(BF16)
    high = jnp.where(lane < HALF, 0.0, both).astype(BF16)
    for p in range(2):
        spare = 0.0
        for k, part in enumerate((low, high)):
            first = (to == R) & (slot_row == 2 * p + k)
            second = (to == R + 1) & (slot_row == 4 + 2 * p + k)
            spare = spare + dot(ones(first | second), part)
        number = 0.0
        if p == 1:
            for k in range(2):
                at = (source[k] - (buoy - 1) * BD) * BD + target[k] - buoy * BD
                at = jnp.where(live[k] == 1, jnp.clip(at, 0, EMPTY), EMPTY)
                number = jnp.where((brow == BLK - 1) & (blane == k), at.astype(F32), number)
        copies[1 + p].wait()
        for q in range(3):
            part = dot(pad, t_ref[p, :, 128 * q : 128 * (q + 1)]).reshape(CHIPS, BLK, 128)
            extra = spare[:, 128 * q : 128 * (q + 1)]
            if p == 1 and q == 2:
                extra = extra + number
            at = 512 * p + 128 * q
            out_ref[:, :, at : at + 128] = (part + extra[None]).astype(BF16)
        last = dot(t_ref[p, :, 384:M], widen).astype(BF16)
        extra = dot(spare[:, 384:M].astype(BF16), widen)
        part = dot(pad, last).reshape(CHIPS, BLK, 128) + extra[None]
        out_ref[:, :, 512 * p + 384 : 512 * p + 512] = part.astype(BF16)


def begin_kernel(where_am_i, own_ref, other_ref, in_ref, out_ref):
    del in_ref
    field = chip_field(own_ref[...], other_ref[...], where_am_i[0], False)
    block = packed(field)
    lane = iota((BLK, 128), 1)
    corner = (
        dot(block, shift(128, 128, 0, 64, 64)),
        jnp.where(lane >= 64, block.astype(F32), 0.0),
    )
    for p in range(2):
        at = 512 * p + 384
        tile = out_ref[:, :, at : at + 128].astype(F32) + corner[p][None]
        out_ref[:, :, at : at + 128] = tile.astype(BF16)


def first_kernel(in_ref, out_ref):
    third = in_ref[:, :, 384:512].reshape(ROWS, 128)
    last = in_ref[:, :, 896:1024].reshape(ROWS, 128)
    lane = iota((ROWS, 128), 1)
    block = dot(third, shift(128, 128, 64, 0, 64)) + jnp.where(lane >= 64, last.astype(F32), 0.0)
    out_ref[...] = block.astype(BF16)


def place_kernel(
    where_am_i, own_at, other_at, in_ref, other_ref, amb_ref, amb_other_ref, w_ref, a_ref, d_ref
):
    core = where_am_i[0]
    w_ref[...] = jnp.zeros_like(w_ref)
    for j in range(CHIPS):
        for p in range(2):
            w_ref[own_at[j, p]] = in_ref[j, :, 512 * p : 512 * (p + 1)]
            w_ref[other_at[j, p]] = other_ref[j, :, 512 * p : 512 * (p + 1)]
    a_ref[...] = chip_field(amb_ref[...], amb_other_ref[...], core, True)
    to, col = iota((ROWS, CHIPS * 8), 0), iota((ROWS, CHIPS * 8), 1)
    same = (to >> 4) == (col >> 3)
    spot = (to & 15, (col & 7) - 6)
    halves = [0.0, 0.0]
    for ref, place in ((in_ref, core), (other_ref, 1 - core)):
        for p in range(2):
            part = ref[:, 8:, 512 * p : 512 * p + M].reshape(CHIPS * 8, M)
            for k in range(2):
                line = spot[0] - S * place - 2 * p - k
                pick = ones(same & (((line == 0) & (spot[1] == 0)) | ((line == 4) & (spot[1] == 1))))
                if p == 1 and k == 1:
                    pick = ones(same & (line == 0) & (spot[1] == 0))
                halves[k] = halves[k] + dot(pick, part)
    d_ref[...] = (
        dot(halves[0].astype(BF16), shift(M, L, 0, 0, HALF))
        + dot(halves[1].astype(BF16), shift(M, L, HALF, 0, HALF))
    ).astype(BF16)


def weighted(w_ref, group, field):
    lane = iota((BD * BLK, L), 1)
    total = jnp.zeros((BD * BLK, L), F32)
    for b in range(BD):
        part = dot(w_ref[BD * group + b, :, :M], field)
        total = total + jnp.where((lane & 7) == b, part, 0.0)
    return total


def own_kernel(w_ref, own_ref, out_ref):
    out_ref[...] = weighted(w_ref, 1, unpacked(own_ref[...]))


def incident_kernel(w_ref, low_ref, high_ref, part_ref, a_ref, out_ref):
    total = part_ref[...]
    total = total + weighted(w_ref, 0, unpacked(low_ref[...]))
    total = total + weighted(w_ref, 2, unpacked(high_ref[...]))
    row, col = iota((L, L), 0), iota((L, L), 1)
    same = ones(((row >> 3) == (col >> 3)) & (row < LAN)).astype(F32)
    total = dot(total, same, exact=True)
    row, lane = iota((BLK, L), 0), iota((BLK, L), 1)
    mine = a_ref[...]
    for t in range(BD):
        mine = mine + jnp.where((lane & 7) == t, total[BLK * t : BLK * (t + 1)], 0.0)
    mine = jnp.where((row < R) & (lane < LAN), mine, 0.0)
    out_ref[...] = jnp.broadcast_to(packed(mine)[None], (CHIPS, BLK, 128))


def coeffs_kernel(where_am_i, in_ref, d_ref, d_other_ref, out_ref):
    field = unpacked(in_ref[...].reshape(ROWS, 128))
    even = (where_am_i[1] & 1) == 0
    upper, lower = field[:HALF].astype(F32), field[HALF:].astype(F32)
    first = jnp.where(even, upper, lower).astype(BF16)
    second = jnp.where(even, lower, upper).astype(BF16)
    out_ref[...] = packed(dot(d_ref[:, :HALF], first) + dot(d_other_ref[:, :HALF], second))


def last_kernel(in_ref, p_ref, d_ref, src_ref, out_ref):
    out = 0.0
    for c in range(C):
        field = unpacked(in_ref[c].reshape(ROWS, 128))
        part = dot(field, p_ref[...], dims=(0, 0))
        src_ref[LAN * c : LAN * (c + 1), :] = part[:LAN].astype(BF16)
        row, col = iota((L, BD * 128), 0), iota((L, BD * 128), 1)
        to = (row & 7) * 128 + (row >> 3) + HC * c
        wide = dot(field, ones((col == to) & (row < LAN))).astype(BF16)
        out = out + dot(d_ref[...], wide)
    for b in range(BD):
        out_ref[:, b, :] = out[:, 128 * b : 128 * b + H]


VM = pl.BlockSpec(memory_space=pltpu.VMEM)
SM = pl.BlockSpec(memory_space=pltpu.SMEM)
HBM = pl.BlockSpec(memory_space=pl.ANY)


def call(kernel, scalars, arrays, shapes, name, **kwargs):
    return pl.pallas_call(
        kernel,
        out_shape=shapes,
        in_specs=[SM] * len(scalars) + [VM] * len(arrays),
        out_specs=[VM] * len(shapes) if isinstance(shapes, tuple) else VM,
        compiler_params=pltpu.CompilerParams(vmem_limit_bytes=40 << 20),
        name=name,
        **kwargs,
    )(*scalars, *arrays)


def shape(*dims, dtype=BF16):
    return jax.ShapeDtypeStruct(dims, dtype)


def exchange(blocks):
    return lax.all_to_all(blocks, PLANE, 0, 0, tiled=True)


def swapped(value):
    return lax.ppermute(value, "c", [(0, 1), (1, 0)])


def from_previous(value):
    count = lax.axis_size("x")
    return lax.ppermute(value, "x", [(i, (i + 1) % count) for i in range(count)])


def from_next(value):
    count = lax.axis_size("x")
    return lax.ppermute(value, "x", [((i + 1) % count, i) for i in range(count)])


def slot_numbers(blocks):
    return blocks[:, BLK - 1, 768:770].astype(I32)


def shards(
    ambient, initial_out, translation, pair_source, pair_target, pair_live, diffract, panel_rows
):
    where_am_i = jnp.stack([lax.axis_index("c"), lax.axis_index("x")]).astype(I32)
    begin = initial_out.transpose(2, 0, 1)
    waves = ambient.transpose(2, 0, 1)
    begin_other = swapped(begin)
    message = pl.pallas_call(
        send_kernel,
        out_shape=shape(CHIPS, BLK, 1024),
        in_specs=[SM] * 4 + [HBM] * 2,
        out_specs=VM,
        scratch_shapes=[
            pltpu.VMEM(translation.shape, BF16),
            pltpu.VMEM(diffract.shape, BF16),
            pltpu.SemaphoreType.DMA((3,)),
        ],
        compiler_params=pltpu.CompilerParams(vmem_limit_bytes=40 << 20),
        name="send",
    )(where_am_i, pair_source, pair_target, pair_live, translation, diffract)
    message = call(
        begin_kernel,
        (where_am_i,),
        (begin, begin_other, message),
        shape(CHIPS, BLK, 1024),
        "begin",
        input_output_aliases={3: 0},
    )
    got = exchange(message)
    got, waves, panel_rows = lax.optimization_barrier((got, waves, panel_rows))
    coeffs = call(first_kernel, (), (got,), shape(ROWS, 128), "first")
    low, high = from_previous(coeffs), from_next(coeffs)
    got_other = swapped(got)
    matrices, own_waves, half = call(
        place_kernel,
        (where_am_i, slot_numbers(got), slot_numbers(got_other)),
        (got, got_other, waves, swapped(waves)),
        (shape(EMPTY + BD, BLK, 512), shape(BLK, L, dtype=F32), shape(ROWS, L)),
        "place",
    )
    matrices = matrices.reshape(SOURCES + 1, BD * BLK, 512)
    other_half = from_previous(half)

    for step in range(ITERS):
        if step:
            coeffs = call(
                coeffs_kernel, (where_am_i,), (got, half, other_half), shape(ROWS, 128), "coeffs"
            )
            low, high = from_previous(coeffs), from_next(coeffs)
        part = call(own_kernel, (), (matrices, coeffs), shape(BD * BLK, L, dtype=F32), "own")
        message = call(
            incident_kernel,
            (),
            (matrices, low, high, part, own_waves),
            shape(CHIPS, BLK, 128),
            "incident",
        )
        got = exchange(message)
    whole = lax.all_gather(got, "c", axis=0, tiled=False)
    sources, outgoing = call(
        last_kernel,
        (),
        (whole, panel_rows.T, diffract),
        (shape(H * BD, panel_rows.shape[0]), shape(S, BD, H, dtype=F32)),
        "last",
    )
    sources = sources.reshape(H, BD, panel_rows.shape[0]).transpose(1, 0, 2)
    return outgoing.transpose(1, 2, 0), sources


def solution(mesh):
    fine = Mesh(mesh.devices.reshape(mesh.shape["buoy"], Z, Y, C), ("x", "z", "y", "c"))
    dom = ("z", "y", "c")
    in_specs = (
        P("x", None, dom),
        P("x", None, dom),
        P(("x",) + dom, None, None),
        P(("x",) + dom),
        P(("x",) + dom),
        P(("x",) + dom),
        P(dom, None),
        P(dom, None),
    )
    out_specs = (P("x", None, dom), P("x", None, dom))
    return jax.shard_map(shards, mesh=fine, in_specs=in_specs, out_specs=out_specs, check_vma=False)
```

```python
import jax
import jax.numpy as jnp
from jax import lax
from jax.experimental import pallas as pl
from jax.experimental.pallas import tpu as pltpu
from jax.sharding import Mesh, PartitionSpec as P

ITERS = 2
Z, Y, C = 8, 4, 2
PLANE = ("z", "y")
CHIPS = Z * Y
F32, BF16, I32 = jnp.float32, jnp.bfloat16, jnp.int32

BD, H, S, M = 8, 36, 7, 448
HC, R, BLK, L = H // C, S * C, 16, 256
LAN = HC * BD
ROWS = CHIPS * BLK
HALF = M // C
SOURCES = 3 * BD
EMPTY = SOURCES * BD


def iota(shape, dim):
    return lax.broadcasted_iota(I32, shape, dim)


def ones(cond):
    return jnp.where(cond, 1.0, 0.0).astype(BF16)


def dot(left, right, dims=(1, 0), exact=False):
    return lax.dot_general(
        left,
        right,
        (((dims[0],), (dims[1],)), ((), ())),
        preferred_element_type=F32,
        precision=lax.Precision.HIGHEST if exact else None,
    )


def shift(rows, cols, start, to, width):
    row, col = iota((rows, cols), 0), iota((rows, cols), 1)
    return ones((row - start == col - to) & (col >= to) & (col < to + width))


def padding():
    row, col = iota((ROWS, M), 0), iota((ROWS, M), 1)
    return ones((col == row - 2 * (row >> 4)) & ((row & 15) < R))


def packing():
    row, col = iota((M, ROWS), 0), iota((M, ROWS), 1)
    return ones((row == col - 2 * (col >> 4)) & ((col & 15) < R))


def two_terms(value):
    high = value.astype(BF16)
    return high, (value - high.astype(F32)).astype(BF16)


def blocks_iota(rows):
    dims = (rows // BLK, BLK, 128)
    return iota(dims, 1), iota(dims, 2)


def packed(field):
    rows = field.shape[0]
    frow, fcol = iota((128, 128), 0), iota((128, 128), 1)
    tail = dot(field[:, 128:].astype(BF16), ones(frow == (fcol & 15))).reshape(-1, BLK, 128)
    row, lane = blocks_iota(rows)
    tail = jnp.where(((lane >> 4) == (row & 7)) & (row < R), tail, 0.0)
    low = jnp.sum(tail[:, :8], axis=1, keepdims=True)
    high = jnp.sum(tail[:, 8:], axis=1, keepdims=True)
    main = field[:, :128].reshape(-1, BLK, 128)
    return jnp.where(row < R, main, jnp.where(row == R, low, high)).astype(BF16)


def unpacked(blocks):
    blocks = blocks.astype(F32)
    row, lane = blocks_iota(ROWS)
    tail = jnp.where(row < 8, blocks[:, R : R + 1], blocks[:, R + 1 :])
    tail = jnp.where(((lane >> 4) == (row & 7)) & (row < R), tail, 0.0)
    frow, fcol = iota((128, 128), 0), iota((128, 128), 1)
    fold = ones((fcol == (frow & 15)) & (fcol < 16))
    tail = dot(tail.reshape(ROWS, 128).astype(BF16), fold)
    main = jnp.where(row < R, blocks, 0.0).reshape(ROWS, 128)
    return jnp.concatenate([main, tail], axis=1).astype(BF16)


def chip_field(own, other, core, exact):
    kind = F32 if exact else BF16
    head, lane = iota((H, L), 0), iota((H, L), 1)
    spread = ones((head == core * HC + (lane >> 3)) & (lane < LAN)).astype(kind)
    row, lane = iota((S * BD, L), 0), iota((S * BD, L), 1)
    total = 0.0
    for value, place in ((own, core), (other, 1 - core)):
        wide = dot(value.reshape(S * BD, H).astype(kind), spread, exact=exact)
        wide = jnp.where((row & 7) == (lane & 7), wide, 0.0)
        to, col = iota((BLK, S * BD), 0), iota((BLK, S * BD), 1)
        gather = ones((col >> 3) == to - S * place).astype(kind)
        total = total + dot(gather, wide.astype(kind), exact=exact)
    return total


def send_kernel(
    where_am_i, source_hbm, target_hbm, live_hbm, t_hbm, d_hbm, begin_hbm, out_ref, begin_ref, t_ref, d_ref,
    source, target, live, sems
):
    moves = ((d_hbm, d_ref), (t_hbm.at[0], t_ref.at[0]), (t_hbm.at[1], t_ref.at[1]), (begin_hbm, begin_ref))
    moves += ((source_hbm, source), (target_hbm, target), (live_hbm, live))
    copies = [pltpu.make_async_copy(a, b, sems.at[i]) for i, (a, b) in enumerate(moves)]
    for copy in copies:
        copy.start()
    buoy = where_am_i[1]
    pad, pack = padding(), packing()
    row, col = iota((M, L), 0), iota((M, L), 1)
    half = ones((row == HALF * (buoy & 1) + col - 2 * (col >> 4)) & ((col & 15) < R))
    to, line = iota((BLK, S), 0), iota((BLK, S), 1)
    brow, blane = iota((BLK, L), 0), iota((BLK, L), 1)
    for i in (0, 4, 5, 6):
        copies[i].wait()
    number = 0.0
    for k in range(2):
        at = (source[k] - (buoy - 1) * BD) * BD + target[k] - buoy * BD
        at = jnp.where(live[k] == 1, jnp.clip(at, 0, EMPTY), EMPTY)
        number = jnp.where((brow == BLK - 1) & (blane == k), at.astype(F32), number)
    own = dot(d_ref[...], half).astype(BF16)
    for p in range(2):
        copies[1 + p].wait()
        wide = dot(t_ref[p], pack).astype(BF16)
        for k in range(2):
            spare = ((to == R) & (line == 2 * p + k)) | ((to == R + 1) & (line == 4 + 2 * p + k))
            extra = dot(ones(spare), own)
            if p == 1 and k == 1:
                extra = extra + number
            part = dot(pad, wide[:, L * k : L * (k + 1)]).reshape(CHIPS, BLK, L) + extra[None]
            at = 512 * p + L * k
            out_ref[:, :, at : at + L] = part.astype(BF16)
    copies[3].wait()


def gaps(p, rows, dim):
    dims = (rows, 128) if dim == 0 else (128, rows)
    place, lane = iota(dims, dim), iota(dims, 1 - dim)
    return ones((lane == 64 * p + 2 * (place >> 4) + (place & 15) - R) & ((place & 15) >= R))


def begin_kernel(where_am_i, own_ref, other_ref, in_ref, out_ref):
    del in_ref
    field = chip_field(own_ref[...], other_ref[...], where_am_i[0], False)
    block = packed(field).reshape(BLK, 128)
    for p in range(2):
        extra = dot(block, gaps(p, 512, 1)).astype(BF16)
        at = 512 * p
        out_ref[:, :, at : at + 512] = out_ref[:, :, at : at + 512] + extra[None]


def first_kernel(in_ref, out_ref):
    block = 0.0
    for p in range(2):
        part = in_ref[:, :, 512 * p : 512 * (p + 1)].reshape(ROWS, 512)
        block = block + dot(part, gaps(p, 512, 0))
    out_ref[...] = block.reshape(CHIPS, BLK, 128).astype(BF16)


def place_kernel(
    where_am_i, own_at, other_at, in_ref, other_ref, amb_ref, amb_other_ref, w_ref, a_ref, d_ref
):
    core = where_am_i[0]
    w_ref[...] = jnp.zeros_like(w_ref)
    for j in range(CHIPS):
        for p in range(2):
            w_ref[own_at[j, 0, p]] = in_ref[j, :, 512 * p : 512 * (p + 1)]
            w_ref[other_at[j, 0, p]] = other_ref[j, :, 512 * p : 512 * (p + 1)]
    a_ref[...] = chip_field(amb_ref[...], amb_other_ref[...], core, True)
    to, col = iota((ROWS, CHIPS * 8), 0), iota((ROWS, CHIPS * 8), 1)
    key = jnp.where((to >> 4) == (col >> 3), (to & 15) * 8 + (col & 7), -1)
    total = 0.0
    for ref, place in ((in_ref, core), (other_ref, 1 - core)):
        for q in range(4):
            part = ref[:, 8:, L * q : L * (q + 1)].reshape(CHIPS * 8, L)
            pick = key == 8 * (S * place + q) + 6
            if q < 3:
                pick = pick | (key == 8 * (S * place + q + 4) + 7)
            total = total + dot(ones(pick), part)
    d_ref[...] = total.astype(BF16)


def weighted(w_ref, group, field):
    lane = iota((BD * BLK, L), 1)
    total = jnp.zeros((BD * BLK, L), F32)
    for b in range(BD):
        part = dot(w_ref[BD * group + b], field)
        total = total + jnp.where((lane & 7) == b, part, 0.0)
    return total


def own_kernel(w_ref, own_ref, out_ref):
    out_ref[...] = weighted(w_ref, 1, unpacked(own_ref[...]))


def incident_kernel(w_ref, low_ref, high_ref, part_ref, a_ref, out_ref):
    total = part_ref[...]
    total = total + weighted(w_ref, 0, unpacked(low_ref[...]))
    total = total + weighted(w_ref, 2, unpacked(high_ref[...]))
    row, col = iota((L, L), 0), iota((L, L), 1)
    same = ones(((row >> 3) == (col >> 3)) & (row < LAN))
    high, rest = two_terms(total)
    total = dot(high, same) + dot(rest, same)
    row, lane = iota((BLK, L), 0), iota((BLK, L), 1)
    mine = a_ref[...]
    for t in range(BD):
        mine = mine + jnp.where((lane & 7) == t, total[BLK * t : BLK * (t + 1)], 0.0)
    mine = jnp.where((row < R) & (lane < LAN), mine, 0.0)
    out_ref[...] = jnp.broadcast_to(packed(mine), (CHIPS, BLK, 128))


def coeffs_kernel(where_am_i, in_ref, d_ref, d_other_ref, out_ref):
    field = unpacked(in_ref[...])
    even = (where_am_i[1] & 1) == 0
    upper, lower = field[:L].astype(F32), field[L:].astype(F32)
    first = jnp.where(even, upper, lower).astype(BF16)
    second = jnp.where(even, lower, upper).astype(BF16)
    out_ref[...] = packed(dot(d_ref[...], first) + dot(d_other_ref[...], second))


def ready_kernel(p_ref, d_ref, p_out, d_out, lanes_out):
    p_out[...] = dot(padding(), p_ref[...]).astype(BF16)
    d_out[...] = dot(d_ref[...], packing()).astype(BF16)
    row, col = iota((L, BD * 128), 0), iota((L, BD * 128), 1)
    to = (row & 7) * 128 + (row >> 3)
    for c in range(C):
        lanes_out[c] = ones((col == to + HC * c) & (row < LAN))


def last_kernel(in_ref, p_ref, d_ref, lanes_ref, src_ref, out_ref):
    out = 0.0
    for c in range(C):
        field = unpacked(in_ref[c])
        part = dot(field, p_ref[...], dims=(0, 0))
        src_ref[LAN * c : LAN * (c + 1), :] = part[:LAN].astype(BF16)
        value = dot(d_ref[...], field)
        for _ in range(3):
            term = value.astype(BF16)
            value = value - term.astype(F32)
            out = out + dot(term, lanes_ref[c])
    for b in range(BD):
        out_ref[:, b, :] = out[:, 128 * b : 128 * b + H]


VM = pl.BlockSpec(memory_space=pltpu.VMEM)
SM = pl.BlockSpec(memory_space=pltpu.SMEM)
HBM = pl.BlockSpec(memory_space=pltpu.HBM)


def call(kernel, scalars, arrays, shapes, name, **kwargs):
    return pl.pallas_call(
        kernel,
        out_shape=shapes,
        in_specs=[SM] * len(scalars) + [VM] * len(arrays),
        out_specs=[VM] * len(shapes) if isinstance(shapes, tuple) else VM,
        compiler_params=pltpu.CompilerParams(vmem_limit_bytes=40 << 20),
        name=name,
        **kwargs,
    )(*scalars, *arrays)


def shape(*dims, dtype=BF16):
    return jax.ShapeDtypeStruct(dims, dtype)


def exchange(blocks):
    return lax.all_to_all(blocks, PLANE, 0, 0, tiled=True)


def swapped(value):
    return lax.ppermute(value, "c", [(0, 1), (1, 0)])


def from_previous(value):
    count = lax.axis_size("x")
    return lax.ppermute(value, "x", [(i, (i + 1) % count) for i in range(count)])


def from_next(value):
    count = lax.axis_size("x")
    return lax.ppermute(value, "x", [((i + 1) % count, i) for i in range(count)])


def slot_numbers(blocks):
    return blocks[:, BLK - 1 :, 768:770].astype(I32)


def shards(
    ambient, initial_out, translation, pair_source, pair_target, pair_live, diffract, panel_rows
):
    where_am_i = jnp.stack([lax.axis_index("c"), lax.axis_index("x")]).astype(I32)
    begin = initial_out.transpose(2, 0, 1)
    waves = ambient.transpose(2, 0, 1)
    begin_other = swapped(begin)
    waves_other = swapped(waves)
    message, begin = pl.pallas_call(
        send_kernel,
        out_shape=(shape(CHIPS, BLK, 1024), shape(*begin.shape, dtype=F32)),
        in_specs=[SM] + [HBM] * 6,
        out_specs=[VM] * 2,
        scratch_shapes=[
            pltpu.VMEM(translation.shape, BF16),
            pltpu.VMEM(diffract.shape, BF16),
            pltpu.SMEM(pair_source.shape, I32),
            pltpu.SMEM(pair_source.shape, I32),
            pltpu.SMEM(pair_source.shape, I32),
            pltpu.SemaphoreType.DMA((7,)),
        ],
        compiler_params=pltpu.CompilerParams(vmem_limit_bytes=40 << 20),
        name="send",
    )(
        where_am_i,
        *[
            pltpu.with_memory_space_constraint(value, pltpu.HBM)
            for value in (pair_source, pair_target, pair_live, translation, diffract, begin)
        ],
    )
    message, waves_other = lax.optimization_barrier((message, waves_other))
    message = call(
        begin_kernel,
        (where_am_i,),
        (begin, begin_other, message),
        shape(CHIPS, BLK, 1024),
        "begin",
        input_output_aliases={3: 0},
    )
    got = exchange(message)
    got, waves = lax.optimization_barrier((got, waves))
    coeffs = call(first_kernel, (), (got,), shape(CHIPS, BLK, 128), "first")
    low, high = from_previous(coeffs), from_next(coeffs)
    got_other = swapped(got)
    matrices, own_waves, half = call(
        place_kernel,
        (where_am_i, slot_numbers(got), slot_numbers(got_other)),
        (got, got_other, waves, waves_other),
        (shape(EMPTY + BD, BLK, 512), shape(BLK, L, dtype=F32), shape(ROWS, L)),
        "place",
    )
    matrices = matrices.reshape(SOURCES + 1, BD * BLK, 512)
    other_half = from_previous(half)

    for step in range(ITERS):
        if step:
            coeffs = call(
                coeffs_kernel,
                (where_am_i,),
                (got, half, other_half),
                shape(CHIPS, BLK, 128),
                "coeffs",
            )
            low, high = from_previous(coeffs), from_next(coeffs)
            coeffs, panel_rows, diffract = lax.optimization_barrier((coeffs, panel_rows, diffract))
            ready = call(
                ready_kernel,
                (),
                (panel_rows.T, diffract),
                (shape(ROWS, panel_rows.shape[0]), shape(S, ROWS), shape(C, L, BD * 128)),
                "ready",
            )
            low, ready = lax.optimization_barrier((low, ready))
        part = call(own_kernel, (), (matrices, coeffs), shape(BD * BLK, L, dtype=F32), "own")
        message = call(
            incident_kernel,
            (),
            (matrices, low, high, part, own_waves),
            shape(CHIPS, BLK, 128),
            "incident",
        )
        got = exchange(message)
    whole = lax.all_gather(got, "c", axis=0, tiled=False)
    sources, outgoing = call(
        last_kernel,
        (),
        (whole, *ready),
        (shape(H * BD, panel_rows.shape[0]), shape(S, BD, H, dtype=F32)),
        "last",
    )
    sources = sources.reshape(H, BD, panel_rows.shape[0]).transpose(1, 0, 2)
    return outgoing.transpose(1, 2, 0), sources


def solution(mesh):
    fine = Mesh(mesh.devices.reshape(mesh.shape["buoy"], Z, Y, C), ("x", "z", "y", "c"))
    dom = ("z", "y", "c")
    in_specs = (
        P("x", None, dom),
        P("x", None, dom),
        P(("x",) + dom, None, None),
        P(("x",) + dom),
        P(("x",) + dom),
        P(("x",) + dom),
        P(dom, None),
        P(dom, None),
    )
    out_specs = (P("x", None, dom), P("x", None, dom))
    return jax.shard_map(shards, mesh=fine, in_specs=in_specs, out_specs=out_specs, check_vma=False)
```

```python
import jax
import jax.numpy as jnp
from jax import lax
from jax.experimental import pallas as pl
from jax.experimental.pallas import tpu as pltpu
from jax.sharding import Mesh, PartitionSpec as P

ITERS = 2
Z, Y, C = 8, 4, 2
PLANE = ("z", "y")
CHIPS = Z * Y
F32, BF16, I32 = jnp.float32, jnp.bfloat16, jnp.int32

BD, H, S, M = 8, 36, 7, 448
HC, R, BLK, L = H // C, S * C, 16, 256
LAN = HC * BD
ROWS = CHIPS * BLK
HALF = M // C
SOURCES = 3 * BD
EMPTY = SOURCES * BD


def iota(shape, dim):
    return lax.broadcasted_iota(I32, shape, dim)


def ones(cond):
    return jnp.where(cond, 1.0, 0.0).astype(BF16)


def dot(left, right, dims=(1, 0), exact=False):
    return lax.dot_general(
        left,
        right,
        (((dims[0],), (dims[1],)), ((), ())),
        preferred_element_type=F32,
        precision=lax.Precision.HIGHEST if exact else None,
    )


def shift(rows, cols, start, to, width):
    row, col = iota((rows, cols), 0), iota((rows, cols), 1)
    return ones((row - start == col - to) & (col >= to) & (col < to + width))


def padding():
    row, col = iota((ROWS, M), 0), iota((ROWS, M), 1)
    return ones((col == row - 2 * (row >> 4)) & ((row & 15) < R))


def packing():
    row, col = iota((M, ROWS), 0), iota((M, ROWS), 1)
    return ones((row == col - 2 * (col >> 4)) & ((col & 15) < R))


def two_terms(value):
    high = value.astype(BF16)
    return high, (value - high.astype(F32)).astype(BF16)


def blocks_iota(rows):
    dims = (rows // BLK, BLK, 128)
    return iota(dims, 1), iota(dims, 2)


def packed(field):
    rows = field.shape[0]
    frow, fcol = iota((128, 128), 0), iota((128, 128), 1)
    tail = dot(field[:, 128:].astype(BF16), ones(frow == (fcol & 15))).reshape(-1, BLK, 128)
    row, lane = blocks_iota(rows)
    tail = jnp.where(((lane >> 4) == (row & 7)) & (row < R), tail, 0.0)
    low = jnp.sum(tail[:, :8], axis=1, keepdims=True)
    high = jnp.sum(tail[:, 8:], axis=1, keepdims=True)
    main = field[:, :128].reshape(-1, BLK, 128)
    return jnp.where(row < R, main, jnp.where(row == R, low, high)).astype(BF16)


def unpacked(blocks):
    blocks = blocks.astype(F32)
    row, lane = blocks_iota(ROWS)
    tail = jnp.where(row < 8, blocks[:, R : R + 1], blocks[:, R + 1 :])
    tail = jnp.where(((lane >> 4) == (row & 7)) & (row < R), tail, 0.0)
    frow, fcol = iota((128, 128), 0), iota((128, 128), 1)
    fold = ones((fcol == (frow & 15)) & (fcol < 16))
    tail = dot(tail.reshape(ROWS, 128).astype(BF16), fold)
    main = jnp.where(row < R, blocks, 0.0).reshape(ROWS, 128)
    return jnp.concatenate([main, tail], axis=1).astype(BF16)


def chip_field(own, other, core, exact):
    kind = F32 if exact else BF16
    head, lane = iota((H, L), 0), iota((H, L), 1)
    spread = ones((head == core * HC + (lane >> 3)) & (lane < LAN)).astype(kind)
    row, lane = iota((S * BD, L), 0), iota((S * BD, L), 1)
    total = 0.0
    for value, place in ((own, core), (other, 1 - core)):
        wide = dot(value.reshape(S * BD, H).astype(kind), spread, exact=exact)
        wide = jnp.where((row & 7) == (lane & 7), wide, 0.0)
        to, col = iota((BLK, S * BD), 0), iota((BLK, S * BD), 1)
        gather = ones((col >> 3) == to - S * place).astype(kind)
        total = total + dot(gather, wide.astype(kind), exact=exact)
    return total


def send_kernel(
    where_am_i, source_hbm, target_hbm, live_hbm, t_hbm, d_hbm, begin_hbm, out_ref, begin_ref, t_ref, d_ref,
    source, target, live, sems
):
    moves = ((d_hbm, d_ref), (t_hbm.at[0], t_ref.at[0]), (t_hbm.at[1], t_ref.at[1]), (begin_hbm, begin_ref))
    moves += ((source_hbm, source), (target_hbm, target), (live_hbm, live))
    copies = [pltpu.make_async_copy(a, b, sems.at[i]) for i, (a, b) in enumerate(moves)]
    for copy in copies:
        copy.start()
    buoy = where_am_i[1]
    pad, pack = padding(), packing()
    row, col = iota((M, L), 0), iota((M, L), 1)
    half = ones((row == HALF * (buoy & 1) + col - 2 * (col >> 4)) & ((col & 15) < R))
    to, line = iota((BLK, S), 0), iota((BLK, S), 1)
    brow, blane = iota((BLK, L), 0), iota((BLK, L), 1)
    for i in (0, 4, 5, 6):
        copies[i].wait()
    number = 0.0
    for k in range(2):
        at = (source[k] - (buoy - 1) * BD) * BD + target[k] - buoy * BD
        at = jnp.where(live[k] == 1, jnp.clip(at, 0, EMPTY), EMPTY)
        number = jnp.where((brow == BLK - 1) & (blane == k), at.astype(F32), number)
    own = dot(d_ref[...], half).astype(BF16)
    for p in range(2):
        copies[1 + p].wait()
        wide = dot(t_ref[p], pack).astype(BF16)
        for k in range(2):
            spare = ((to == R) & (line == 2 * p + k)) | ((to == R + 1) & (line == 4 + 2 * p + k))
            extra = dot(ones(spare), own)
            if p == 1 and k == 1:
                extra = extra + number
            part = dot(pad, wide[:, L * k : L * (k + 1)]).reshape(CHIPS, BLK, L) + extra[None]
            at = 512 * p + L * k
            out_ref[:, :, at : at + L] = part.astype(BF16)
    copies[3].wait()


def gaps(p, rows, dim):
    dims = (rows, 128) if dim == 0 else (128, rows)
    place, lane = iota(dims, dim), iota(dims, 1 - dim)
    return ones((lane == 64 * p + 2 * (place >> 4) + (place & 15) - R) & ((place & 15) >= R))


def begin_kernel(where_am_i, own_ref, other_ref, in_ref, out_ref):
    del in_ref
    field = chip_field(own_ref[...], other_ref[...], where_am_i[0], False)
    block = packed(field).reshape(BLK, 128)
    for p in range(2):
        extra = dot(block, gaps(p, 512, 1)).astype(BF16)
        at = 512 * p
        out_ref[:, :, at : at + 512] = out_ref[:, :, at : at + 512] + extra[None]


def first_kernel(in_ref, out_ref):
    block = 0.0
    for p in range(2):
        part = in_ref[:, :, 512 * p : 512 * (p + 1)].reshape(ROWS, 512)
        block = block + dot(part, gaps(p, 512, 0))
    out_ref[...] = block.reshape(CHIPS, BLK, 128).astype(BF16)


def place_kernel(
    where_am_i, own_at, other_at, in_ref, other_ref, amb_ref, amb_other_ref, w_ref, a_ref, d_ref
):
    core = where_am_i[0]
    w_ref[...] = jnp.zeros_like(w_ref)
    for j in range(CHIPS):
        for p in range(2):
            w_ref[own_at[j, 0, p]] = in_ref[j, :, 512 * p : 512 * (p + 1)]
            w_ref[other_at[j, 0, p]] = other_ref[j, :, 512 * p : 512 * (p + 1)]
    a_ref[...] = chip_field(amb_ref[...], amb_other_ref[...], core, True)
    part_rows, width = 8 * BLK, 4 * 64
    to, col = iota((part_rows, width), 0), iota((part_rows, width), 1)
    line = (to & 15) - (col >> 6)
    picks = []
    for place in (core, 1 - core):
        upper = (line == S * place) & ((col & 7) == 6)
        lower = (line == S * place + 4) & ((col & 7) == 7) & ((col >> 6) < 3)
        picks.append(ones(((to >> 4) == ((col >> 3) & 7)) & (upper | lower)))
    for g in range(CHIPS // 8):
        total = 0.0
        for ref, pick in zip((in_ref, other_ref), picks):
            cells = [
                ref[8 * g : 8 * (g + 1), 8:, L * q : L * (q + 1)].reshape(64, L) for q in range(4)
            ]
            total = total + dot(pick, jnp.concatenate(cells, axis=0))
        d_ref[part_rows * g : part_rows * (g + 1), :] = total.astype(BF16)


def weighted(w_ref, group, field):
    lane = iota((BD * BLK, L), 1)
    total = jnp.zeros((BD * BLK, L), F32)
    for b in range(BD):
        part = dot(w_ref[BD * group + b], field)
        total = total + jnp.where((lane & 7) == b, part, 0.0)
    return total


def own_kernel(w_ref, own_ref, out_ref):
    out_ref[...] = weighted(w_ref, 1, unpacked(own_ref[...]))


def incident_kernel(w_ref, low_ref, high_ref, part_ref, a_ref, out_ref):
    total = part_ref[...]
    total = total + weighted(w_ref, 0, unpacked(low_ref[...]))
    total = total + weighted(w_ref, 2, unpacked(high_ref[...]))
    row, col = iota((L, L), 0), iota((L, L), 1)
    same = ones(((row >> 3) == (col >> 3)) & (row < LAN))
    high, rest = two_terms(total)
    total = dot(high, same) + dot(rest, same)
    row, lane = iota((BLK, L), 0), iota((BLK, L), 1)
    mine = a_ref[...]
    for t in range(BD):
        mine = mine + jnp.where((lane & 7) == t, total[BLK * t : BLK * (t + 1)], 0.0)
    mine = jnp.where((row < R) & (lane < LAN), mine, 0.0)
    out_ref[...] = jnp.broadcast_to(packed(mine), (CHIPS, BLK, 128))


def product_kernel(where_am_i, w_ref, d_ref, d_other_ref, out_ref):
    even = (where_am_i[1] & 1) == 0
    own, other = d_ref[...].astype(F32), d_other_ref[...].astype(F32)
    halves = (
        jnp.where(even, own, other).astype(BF16),
        jnp.where(even, other, own).astype(BF16),
    )
    for s in range(SOURCES):
        for k in range(2):
            out_ref[s, :, L * k : L * (k + 1)] = dot(w_ref[s], halves[k]).astype(BF16)


def ready_kernel(p_ref, d_ref, p_out, d_out, lanes_out):
    p_out[...] = dot(padding(), p_ref[...]).astype(BF16)
    d_out[...] = dot(d_ref[...], packing()).astype(BF16)
    row, col = iota((L, BD * 128), 0), iota((L, BD * 128), 1)
    to = (row & 7) * 128 + (row >> 3)
    for c in range(C):
        lanes_out[c] = ones((col == to + HC * c) & (row < LAN))


def outputs(blocks, p_ref, d_ref, lanes):
    field = unpacked(blocks)
    sources = dot(field, p_ref[...], dims=(0, 0))[:LAN].astype(BF16)
    high, rest = two_terms(dot(d_ref[...], field))
    return sources, dot(high, lanes) + dot(rest, lanes)


def last_own_kernel(where_am_i, in_ref, p_ref, d_ref, lanes_ref, src_ref, out_ref):
    src_ref[...], out_ref[...] = outputs(in_ref[...], p_ref, d_ref, lanes_ref[where_am_i[0]])


def last_kernel(
    where_am_i, in_ref, p_ref, d_ref, lanes_ref, own_src_ref, own_out_ref, src_ref, out_ref
):
    core = where_am_i[0]
    other, out = outputs(in_ref[...], p_ref, d_ref, lanes_ref[1 - core])
    out = out + own_out_ref[...]
    src_ref[pl.ds(pl.multiple_of(LAN * core, BLK), LAN), :] = own_src_ref[...]
    src_ref[pl.ds(pl.multiple_of(LAN * (1 - core), BLK), LAN), :] = other
    for b in range(BD):
        out_ref[:, b, :] = out[:, 128 * b : 128 * b + H]


VM = pl.BlockSpec(memory_space=pltpu.VMEM)
SM = pl.BlockSpec(memory_space=pltpu.SMEM)
HBM = pl.BlockSpec(memory_space=pltpu.HBM)


def call(kernel, scalars, arrays, shapes, name, **kwargs):
    return pl.pallas_call(
        kernel,
        out_shape=shapes,
        in_specs=[SM] * len(scalars) + [VM] * len(arrays),
        out_specs=[VM] * len(shapes) if isinstance(shapes, tuple) else VM,
        compiler_params=pltpu.CompilerParams(vmem_limit_bytes=40 << 20),
        name=name,
        **kwargs,
    )(*scalars, *arrays)


def shape(*dims, dtype=BF16):
    return jax.ShapeDtypeStruct(dims, dtype)


def exchange(blocks):
    return lax.all_to_all(blocks, PLANE, 0, 0, tiled=True)


def swapped(value):
    return lax.ppermute(value, "c", [(0, 1), (1, 0)])


def from_previous(value):
    count = lax.axis_size("x")
    return lax.ppermute(value, "x", [(i, (i + 1) % count) for i in range(count)])


def from_next(value):
    count = lax.axis_size("x")
    return lax.ppermute(value, "x", [((i + 1) % count, i) for i in range(count)])


def slot_numbers(blocks):
    return blocks[:, BLK - 1 :, 768:770].astype(I32)


def shards(
    ambient, initial_out, translation, pair_source, pair_target, pair_live, diffract, panel_rows
):
    where_am_i = jnp.stack([lax.axis_index("c"), lax.axis_index("x")]).astype(I32)
    begin = initial_out.transpose(2, 0, 1)
    waves = ambient.transpose(2, 0, 1)
    begin_other = swapped(begin)
    waves_other = swapped(waves)
    message, begin = pl.pallas_call(
        send_kernel,
        out_shape=(shape(CHIPS, BLK, 1024), shape(*begin.shape, dtype=F32)),
        in_specs=[SM] + [HBM] * 6,
        out_specs=[VM] * 2,
        scratch_shapes=[
            pltpu.VMEM(translation.shape, BF16),
            pltpu.VMEM(diffract.shape, BF16),
            pltpu.SMEM(pair_source.shape, I32),
            pltpu.SMEM(pair_source.shape, I32),
            pltpu.SMEM(pair_source.shape, I32),
            pltpu.SemaphoreType.DMA((7,)),
        ],
        compiler_params=pltpu.CompilerParams(vmem_limit_bytes=40 << 20),
        name="send",
    )(
        where_am_i,
        *[
            pltpu.with_memory_space_constraint(value, pltpu.HBM)
            for value in (pair_source, pair_target, pair_live, translation, diffract, begin)
        ],
    )
    message, waves_other = lax.optimization_barrier((message, waves_other))
    message = call(
        begin_kernel,
        (where_am_i,),
        (begin, begin_other, message),
        shape(CHIPS, BLK, 1024),
        "begin",
        input_output_aliases={3: 0},
    )
    got = exchange(message)
    got, waves = lax.optimization_barrier((got, waves))
    coeffs = call(first_kernel, (), (got,), shape(CHIPS, BLK, 128), "first")
    low, high = from_previous(coeffs), from_next(coeffs)
    got_other = swapped(got)
    matrices, own_waves, half = call(
        place_kernel,
        (where_am_i, slot_numbers(got), slot_numbers(got_other)),
        (got, got_other, waves, waves_other),
        (shape(EMPTY + BD, BLK, 512), shape(BLK, L, dtype=F32), shape(ROWS, L)),
        "place",
    )
    matrices = matrices.reshape(SOURCES + 1, BD * BLK, 512)
    other_half = from_previous(half)

    field = coeffs
    for step in range(ITERS):
        if step:
            got, other_half = lax.optimization_barrier((got, other_half))
            field, low, high = got, from_previous(got), from_next(got)
            field, half, panel_rows, diffract = lax.optimization_barrier(
                (field, half, panel_rows, diffract)
            )
            matrices = call(
                product_kernel,
                (where_am_i,),
                (matrices, half, other_half),
                shape(SOURCES, BD * BLK, 512),
                "product",
            )
            ready = call(
                ready_kernel,
                (),
                (panel_rows.T, diffract),
                (shape(ROWS, panel_rows.shape[0]), shape(S, ROWS), shape(C, L, BD * 128)),
                "ready",
            )
            low, ready = lax.optimization_barrier((low, ready))
        part = call(own_kernel, (), (matrices, field), shape(BD * BLK, L, dtype=F32), "own")
        message = call(
            incident_kernel,
            (),
            (matrices, low, high, part, own_waves),
            shape(CHIPS, BLK, 128),
            "incident",
        )
        got = exchange(message)
    other = swapped(got)
    own_sources, own_outgoing = call(
        last_own_kernel,
        (where_am_i,),
        (got, *ready),
        (shape(LAN, panel_rows.shape[0]), shape(S, BD * 128, dtype=F32)),
        "last_own",
    )
    sources, outgoing = call(
        last_kernel,
        (where_am_i,),
        (other, *ready, own_sources, own_outgoing),
        (shape(H * BD, panel_rows.shape[0]), shape(S, BD, H, dtype=F32)),
        "last",
    )
    sources = sources.reshape(H, BD, panel_rows.shape[0]).transpose(1, 0, 2)
    return outgoing.transpose(1, 2, 0), sources


def solution(mesh):
    fine = Mesh(mesh.devices.reshape(mesh.shape["buoy"], Z, Y, C), ("x", "z", "y", "c"))
    dom = ("z", "y", "c")
    in_specs = (
        P("x", None, dom),
        P("x", None, dom),
        P(("x",) + dom, None, None),
        P(("x",) + dom),
        P(("x",) + dom),
        P(("x",) + dom),
        P(dom, None),
        P(dom, None),
    )
    out_specs = (P("x", None, dom), P("x", None, dom))
    return jax.shard_map(shards, mesh=fine, in_specs=in_specs, out_specs=out_specs, check_vma=False)
```

```python
import jax
import jax.numpy as jnp
from jax import lax
from jax.experimental import pallas as pl
from jax.experimental.pallas import tpu as pltpu
from jax.sharding import Mesh, PartitionSpec as P

ITERS = 2
Z, Y, C = 8, 4, 2
PLANE = ("z", "y")
CHIPS = Z * Y
F32, BF16, I32 = jnp.float32, jnp.bfloat16, jnp.int32

BD, H, S, M = 8, 36, 7, 448
HC, R, BLK, L = H // C, S * C, 16, 256
LAN = HC * BD
ROWS = CHIPS * BLK
HALF = M // C
SOURCES = 3 * BD
EMPTY = SOURCES * BD


def iota(shape, dim):
    return lax.broadcasted_iota(I32, shape, dim)


def ones(cond):
    return jnp.where(cond, 1.0, 0.0).astype(BF16)


def dot(left, right, dims=(1, 0), exact=False):
    return lax.dot_general(
        left,
        right,
        (((dims[0],), (dims[1],)), ((), ())),
        preferred_element_type=F32,
        precision=lax.Precision.HIGHEST if exact else None,
    )


def shift(rows, cols, start, to, width):
    row, col = iota((rows, cols), 0), iota((rows, cols), 1)
    return ones((row - start == col - to) & (col >= to) & (col < to + width))


def padding():
    row, col = iota((ROWS, M), 0), iota((ROWS, M), 1)
    return ones((col == row - 2 * (row >> 4)) & ((row & 15) < R))


def packing():
    row, col = iota((M, ROWS), 0), iota((M, ROWS), 1)
    return ones((row == col - 2 * (col >> 4)) & ((col & 15) < R))


def two_terms(value):
    high = value.astype(BF16)
    return high, (value - high.astype(F32)).astype(BF16)


def blocks_iota(rows):
    dims = (rows // BLK, BLK, 128)
    return iota(dims, 1), iota(dims, 2)


def packed(field):
    rows = field.shape[0]
    frow, fcol = iota((128, 128), 0), iota((128, 128), 1)
    tail = dot(field[:, 128:].astype(BF16), ones(frow == (fcol & 15))).reshape(-1, BLK, 128)
    row, lane = blocks_iota(rows)
    tail = jnp.where(((lane >> 4) == (row & 7)) & (row < R), tail, 0.0)
    low = jnp.sum(tail[:, :8], axis=1, keepdims=True)
    high = jnp.sum(tail[:, 8:], axis=1, keepdims=True)
    main = field[:, :128].reshape(-1, BLK, 128)
    return jnp.where(row < R, main, jnp.where(row == R, low, high)).astype(BF16)


def unpacked(blocks):
    blocks = blocks.astype(F32)
    row, lane = blocks_iota(ROWS)
    tail = jnp.where(row < 8, blocks[:, R : R + 1], blocks[:, R + 1 :])
    tail = jnp.where(((lane >> 4) == (row & 7)) & (row < R), tail, 0.0)
    frow, fcol = iota((128, 128), 0), iota((128, 128), 1)
    fold = ones((fcol == (frow & 15)) & (fcol < 16))
    tail = dot(tail.reshape(ROWS, 128).astype(BF16), fold)
    main = jnp.where(row < R, blocks, 0.0).reshape(ROWS, 128)
    return jnp.concatenate([main, tail], axis=1).astype(BF16)


def chip_field(own, other, core, exact):
    kind = F32 if exact else BF16
    head, lane = iota((H, L), 0), iota((H, L), 1)
    spread = ones((head == core * HC + (lane >> 3)) & (lane < LAN)).astype(kind)
    row, lane = iota((S * BD, L), 0), iota((S * BD, L), 1)
    total = 0.0
    for value, place in ((own, core), (other, 1 - core)):
        wide = dot(value.reshape(S * BD, H).astype(kind), spread, exact=exact)
        wide = jnp.where((row & 7) == (lane & 7), wide, 0.0)
        to, col = iota((BLK, S * BD), 0), iota((BLK, S * BD), 1)
        gather = ones((col >> 3) == to - S * place).astype(kind)
        total = total + dot(gather, wide.astype(kind), exact=exact)
    return total


def send_kernel(
    where_am_i, source_hbm, target_hbm, live_hbm, t_hbm, d_hbm, begin_hbm, out_ref, begin_ref, t_ref, d_ref,
    source, target, live, sems
):
    moves = ((d_hbm, d_ref), (t_hbm.at[0], t_ref.at[0]), (t_hbm.at[1], t_ref.at[1]), (begin_hbm, begin_ref))
    moves += ((source_hbm, source), (target_hbm, target), (live_hbm, live))
    copies = [pltpu.make_async_copy(a, b, sems.at[i]) for i, (a, b) in enumerate(moves)]
    for copy in copies:
        copy.start()
    buoy = where_am_i[1]
    pack = packing()
    row, col = iota((M, L), 0), iota((M, L), 1)
    half = ones((row == HALF * (buoy & 1) + col - 2 * (col >> 4)) & ((col & 15) < R))
    to, line = iota((BLK, S), 0), iota((BLK, S), 1)
    brow, blane = iota((BLK, L), 0), iota((BLK, L), 1)
    for i in (0, 4, 5, 6):
        copies[i].wait()
    number = 0.0
    for k in range(2):
        at = (source[k] - (buoy - 1) * BD) * BD + target[k] - buoy * BD
        at = jnp.where(live[k] == 1, jnp.clip(at, 0, EMPTY), EMPTY)
        number = jnp.where((brow == BLK - 1) & (blane == k), at.astype(F32), number)
    own = dot(d_ref[...], half).astype(BF16)
    brow = iota((BLK, 2 * L), 0)
    for p in range(2):
        extra = []
        for k in range(2):
            spare = ((to == R) & (line == 2 * p + k)) | ((to == R + 1) & (line == 4 + 2 * p + k))
            extra.append(dot(ones(spare), own))
        if p == 1:
            extra[1] = extra[1] + number
        extra = jnp.concatenate(extra, axis=1)
        copies[1 + p].wait()
        wide = dot(t_ref[p], pack)
        for j in range(CHIPS):
            rows = wide[R * j : min(R * j + BLK, M)]
            if j == CHIPS - 1:
                rows = jnp.concatenate([rows, jnp.zeros((BLK - R, 2 * L), F32)], axis=0)
            rows = jnp.where(brow < R, rows, extra)
            out_ref[j, :, 2 * L * p : 2 * L * (p + 1)] = rows.astype(BF16)
    copies[3].wait()


def gaps(p, rows, dim):
    dims = (rows, 128) if dim == 0 else (128, rows)
    place, lane = iota(dims, dim), iota(dims, 1 - dim)
    return ones((lane == 64 * p + 2 * (place >> 4) + (place & 15) - R) & ((place & 15) >= R))


def begin_kernel(where_am_i, own_ref, other_ref, in_ref, out_ref):
    del in_ref
    field = chip_field(own_ref[...], other_ref[...], where_am_i[0], False)
    block = packed(field).reshape(BLK, 128)
    for p in range(2):
        extra = dot(block, gaps(p, 512, 1)).astype(BF16)
        at = 512 * p
        out_ref[:, :, at : at + 512] = out_ref[:, :, at : at + 512] + extra[None]


def first_kernel(in_ref, out_ref):
    block = 0.0
    for p in range(2):
        part = in_ref[:, :, 512 * p : 512 * (p + 1)].reshape(ROWS, 512)
        block = block + dot(part, gaps(p, 512, 0))
    out_ref[...] = block.reshape(CHIPS, BLK, 128).astype(BF16)


def place_kernel(
    where_am_i, own_at, other_at, in_ref, other_ref, amb_ref, amb_other_ref, w_ref, a_ref, d_ref
):
    core = where_am_i[0]
    w_ref[...] = jnp.zeros_like(w_ref)
    for j in range(CHIPS):
        for p in range(2):
            w_ref[own_at[j, 0, p]] = in_ref[j, :, 512 * p : 512 * (p + 1)]
            w_ref[other_at[j, 0, p]] = other_ref[j, :, 512 * p : 512 * (p + 1)]
    a_ref[...] = chip_field(amb_ref[...], amb_other_ref[...], core, True)
    part_rows, width = 8 * BLK, 4 * 64
    to, col = iota((part_rows, width), 0), iota((part_rows, width), 1)
    line = (to & 15) - (col >> 6)
    picks = []
    for place in (core, 1 - core):
        upper = (line == S * place) & ((col & 7) == 6)
        lower = (line == S * place + 4) & ((col & 7) == 7) & ((col >> 6) < 3)
        picks.append(ones(((to >> 4) == ((col >> 3) & 7)) & (upper | lower)))
    for g in range(CHIPS // 8):
        total = 0.0
        for ref, pick in zip((in_ref, other_ref), picks):
            cells = [
                ref[8 * g : 8 * (g + 1), 8:, L * q : L * (q + 1)].reshape(64, L) for q in range(4)
            ]
            total = total + dot(pick, jnp.concatenate(cells, axis=0))
        d_ref[part_rows * g : part_rows * (g + 1), :] = total.astype(BF16)


def weighted(w_ref, group, field):
    lane = iota((BD * BLK, L), 1)
    total = jnp.zeros((BD * BLK, L), F32)
    for b in range(BD):
        part = dot(w_ref[BD * group + b], field)
        total = total + jnp.where((lane & 7) == b, part, 0.0)
    return total


def own_kernel(w_ref, own_ref, out_ref):
    out_ref[...] = weighted(w_ref, 1, unpacked(own_ref[...]))


def incident_kernel(w_ref, low_ref, high_ref, part_ref, a_ref, out_ref):
    total = part_ref[...]
    total = total + weighted(w_ref, 0, unpacked(low_ref[...]))
    total = total + weighted(w_ref, 2, unpacked(high_ref[...]))
    row, col = iota((L, L), 0), iota((L, L), 1)
    same = ones(((row >> 3) == (col >> 3)) & (row < LAN))
    high, rest = two_terms(total)
    total = dot(high, same) + dot(rest, same)
    row, lane = iota((BLK, L), 0), iota((BLK, L), 1)
    mine = a_ref[...]
    for t in range(BD):
        mine = mine + jnp.where((lane & 7) == t, total[BLK * t : BLK * (t + 1)], 0.0)
    mine = jnp.where((row < R) & (lane < LAN), mine, 0.0)
    out_ref[...] = jnp.broadcast_to(packed(mine), (CHIPS, BLK, 128))


def coeffs_kernel(where_am_i, in_ref, d_ref, d_other_ref, out_ref):
    field = unpacked(in_ref[...])
    even = (where_am_i[1] & 1) == 0
    upper, lower = field[:L].astype(F32), field[L:].astype(F32)
    first = jnp.where(even, upper, lower).astype(BF16)
    second = jnp.where(even, lower, upper).astype(BF16)
    out_ref[...] = packed(dot(d_ref[...], first) + dot(d_other_ref[...], second))


def ready_kernel(p_ref, d_ref, p_out, d_out, lanes_out):
    p_out[...] = dot(padding(), p_ref[...]).astype(BF16)
    d_out[...] = dot(d_ref[...], packing()).astype(BF16)
    row, col = iota((L, BD * 128), 0), iota((L, BD * 128), 1)
    to = (row & 7) * 128 + (row >> 3)
    for c in range(C):
        lanes_out[c] = ones((col == to + HC * c) & (row < LAN))


def outputs(blocks, p_ref, d_ref, lanes):
    field = unpacked(blocks)
    sources = dot(field, p_ref[...], dims=(0, 0))[:LAN].astype(BF16)
    high, rest = two_terms(dot(d_ref[...], field))
    return sources, dot(high, lanes) + dot(rest, lanes)


def last_own_kernel(where_am_i, in_ref, p_ref, d_ref, lanes_ref, src_ref, out_ref):
    src_ref[...], out_ref[...] = outputs(in_ref[...], p_ref, d_ref, lanes_ref[where_am_i[0]])


def last_kernel(
    where_am_i, in_ref, p_ref, d_ref, lanes_ref, own_src_ref, own_out_ref, src_ref, out_ref
):
    core = where_am_i[0]
    other, out = outputs(in_ref[...], p_ref, d_ref, lanes_ref[1 - core])
    out = out + own_out_ref[...]
    src_ref[pl.ds(pl.multiple_of(LAN * core, BLK), LAN), :] = own_src_ref[...]
    src_ref[pl.ds(pl.multiple_of(LAN * (1 - core), BLK), LAN), :] = other
    for b in range(BD):
        out_ref[:, b, :] = out[:, 128 * b : 128 * b + H]


VM = pl.BlockSpec(memory_space=pltpu.VMEM)
SM = pl.BlockSpec(memory_space=pltpu.SMEM)
HBM = pl.BlockSpec(memory_space=pltpu.HBM)


def call(kernel, scalars, arrays, shapes, name, **kwargs):
    return pl.pallas_call(
        kernel,
        out_shape=shapes,
        in_specs=[SM] * len(scalars) + [VM] * len(arrays),
        out_specs=[VM] * len(shapes) if isinstance(shapes, tuple) else VM,
        compiler_params=pltpu.CompilerParams(vmem_limit_bytes=40 << 20),
        name=name,
        **kwargs,
    )(*scalars, *arrays)


def shape(*dims, dtype=BF16):
    return jax.ShapeDtypeStruct(dims, dtype)


def exchange(blocks):
    return lax.all_to_all(blocks, PLANE, 0, 0, tiled=True)


def swapped(value):
    return lax.ppermute(value, "c", [(0, 1), (1, 0)])


def from_previous(value):
    count = lax.axis_size("x")
    return lax.ppermute(value, "x", [(i, (i + 1) % count) for i in range(count)])


def from_next(value):
    count = lax.axis_size("x")
    return lax.ppermute(value, "x", [((i + 1) % count, i) for i in range(count)])


def slot_numbers(blocks):
    return blocks[:, BLK - 1 :, 768:770].astype(I32)


def shards(
    ambient, initial_out, translation, pair_source, pair_target, pair_live, diffract, panel_rows
):
    where_am_i = jnp.stack([lax.axis_index("c"), lax.axis_index("x")]).astype(I32)
    begin = initial_out.transpose(2, 0, 1)
    waves = ambient.transpose(2, 0, 1)
    begin_other = swapped(begin)
    waves_other = swapped(waves)
    message, begin = pl.pallas_call(
        send_kernel,
        out_shape=(shape(CHIPS, BLK, 1024), shape(*begin.shape, dtype=F32)),
        in_specs=[SM] + [HBM] * 6,
        out_specs=[VM] * 2,
        scratch_shapes=[
            pltpu.VMEM(translation.shape, BF16),
            pltpu.VMEM(diffract.shape, BF16),
            pltpu.SMEM(pair_source.shape, I32),
            pltpu.SMEM(pair_source.shape, I32),
            pltpu.SMEM(pair_source.shape, I32),
            pltpu.SemaphoreType.DMA((7,)),
        ],
        compiler_params=pltpu.CompilerParams(vmem_limit_bytes=40 << 20),
        name="send",
    )(
        where_am_i,
        *[
            pltpu.with_memory_space_constraint(value, pltpu.HBM)
            for value in (pair_source, pair_target, pair_live, translation, diffract, begin)
        ],
    )
    message, waves_other = lax.optimization_barrier((message, waves_other))
    message = call(
        begin_kernel,
        (where_am_i,),
        (begin, begin_other, message),
        shape(CHIPS, BLK, 1024),
        "begin",
        input_output_aliases={3: 0},
    )
    got = exchange(message)
    got, waves = lax.optimization_barrier((got, waves))
    coeffs = call(first_kernel, (), (got,), shape(CHIPS, BLK, 128), "first")
    low, high = from_previous(coeffs), from_next(coeffs)
    got_other = swapped(got)
    matrices, own_waves, half = call(
        place_kernel,
        (where_am_i, slot_numbers(got), slot_numbers(got_other)),
        (got, got_other, waves, waves_other),
        (shape(EMPTY + BD, BLK, 512), shape(BLK, L, dtype=F32), shape(ROWS, L)),
        "place",
    )
    matrices = matrices.reshape(SOURCES + 1, BD * BLK, 512)
    other_half = from_previous(half)

    for step in range(ITERS):
        if step:
            coeffs = call(
                coeffs_kernel,
                (where_am_i,),
                (got, half, other_half),
                shape(CHIPS, BLK, 128),
                "coeffs",
            )
            low, high = from_previous(coeffs), from_next(coeffs)
            coeffs, panel_rows, diffract = lax.optimization_barrier((coeffs, panel_rows, diffract))
            ready = call(
                ready_kernel,
                (),
                (panel_rows.T, diffract),
                (shape(ROWS, panel_rows.shape[0]), shape(S, ROWS), shape(C, L, BD * 128)),
                "ready",
            )
            low, ready = lax.optimization_barrier((low, ready))
        part = call(own_kernel, (), (matrices, coeffs), shape(BD * BLK, L, dtype=F32), "own")
        message = call(
            incident_kernel,
            (),
            (matrices, low, high, part, own_waves),
            shape(CHIPS, BLK, 128),
            "incident",
        )
        got = exchange(message)
    other = swapped(got)
    own_sources, own_outgoing = call(
        last_own_kernel,
        (where_am_i,),
        (got, *ready),
        (shape(LAN, panel_rows.shape[0]), shape(S, BD * 128, dtype=F32)),
        "last_own",
    )
    sources, outgoing = call(
        last_kernel,
        (where_am_i,),
        (other, *ready, own_sources, own_outgoing),
        (shape(H * BD, panel_rows.shape[0]), shape(S, BD, H, dtype=F32)),
        "last",
    )
    sources = sources.reshape(H, BD, panel_rows.shape[0]).transpose(1, 0, 2)
    return outgoing.transpose(1, 2, 0), sources


def solution(mesh):
    fine = Mesh(mesh.devices.reshape(mesh.shape["buoy"], Z, Y, C), ("x", "z", "y", "c"))
    dom = ("z", "y", "c")
    in_specs = (
        P("x", None, dom),
        P("x", None, dom),
        P(("x",) + dom, None, None),
        P(("x",) + dom),
        P(("x",) + dom),
        P(("x",) + dom),
        P(dom, None),
        P(dom, None),
    )
    out_specs = (P("x", None, dom), P("x", None, dom))
    return jax.shard_map(shards, mesh=fine, in_specs=in_specs, out_specs=out_specs, check_vma=False)
```

```python
import functools

import jax
import jax.numpy as jnp
from jax import lax
from jax.experimental import pallas as pl
from jax.experimental.pallas import tpu as pltpu
from jax.sharding import Mesh, PartitionSpec as P

ITERS = 2
Z, Y, C = 8, 4, 2
PLANE = ("z", "y")
CHIPS = Z * Y
F32, BF16, I32 = jnp.float32, jnp.bfloat16, jnp.int32

BD, H, S, M = 8, 36, 7, 448
HC, R, BLK, L = H // C, S * C, 16, 256
LAN = HC * BD
ROWS = CHIPS * BLK
HALF = M // C
SOURCES = 3 * BD
EMPTY = SOURCES * BD


def iota(shape, dim):
    return lax.broadcasted_iota(I32, shape, dim)


def ones(cond):
    return jnp.where(cond, 1.0, 0.0).astype(BF16)


def dot(left, right, dims=(1, 0), exact=False):
    return lax.dot_general(
        left,
        right,
        (((dims[0],), (dims[1],)), ((), ())),
        preferred_element_type=F32,
        precision=lax.Precision.HIGHEST if exact else None,
    )


def shift(rows, cols, start, to, width):
    row, col = iota((rows, cols), 0), iota((rows, cols), 1)
    return ones((row - start == col - to) & (col >= to) & (col < to + width))


def padding():
    row, col = iota((ROWS, M), 0), iota((ROWS, M), 1)
    return ones((col == row - 2 * (row >> 4)) & ((row & 15) < R))


def packing():
    row, col = iota((M, ROWS), 0), iota((M, ROWS), 1)
    return ones((row == col - 2 * (col >> 4)) & ((col & 15) < R))


def two_terms(value):
    high = value.astype(BF16)
    return high, (value - high.astype(F32)).astype(BF16)


def blocks_iota(rows):
    dims = (rows // BLK, BLK, 128)
    return iota(dims, 1), iota(dims, 2)


def packed(field):
    rows = field.shape[0]
    frow, fcol = iota((128, 128), 0), iota((128, 128), 1)
    tail = dot(field[:, 128:].astype(BF16), ones(frow == (fcol & 15))).reshape(-1, BLK, 128)
    row, lane = blocks_iota(rows)
    tail = jnp.where(((lane >> 4) == (row & 7)) & (row < R), tail, 0.0)
    low = jnp.sum(tail[:, :8], axis=1, keepdims=True)
    high = jnp.sum(tail[:, 8:], axis=1, keepdims=True)
    main = field[:, :128].reshape(-1, BLK, 128)
    return jnp.where(row < R, main, jnp.where(row == R, low, high)).astype(BF16)


def unpacked(blocks):
    blocks = blocks.astype(F32)
    row, lane = blocks_iota(ROWS)
    tail = jnp.where(row < 8, blocks[:, R : R + 1], blocks[:, R + 1 :])
    tail = jnp.where(((lane >> 4) == (row & 7)) & (row < R), tail, 0.0)
    frow, fcol = iota((128, 128), 0), iota((128, 128), 1)
    fold = ones((fcol == (frow & 15)) & (fcol < 16))
    tail = dot(tail.reshape(ROWS, 128).astype(BF16), fold)
    main = jnp.where(row < R, blocks, 0.0).reshape(ROWS, 128)
    return jnp.concatenate([main, tail], axis=1).astype(BF16)


def chip_field(own, other, core, exact):
    kind = F32 if exact else BF16
    head, lane = iota((H, L), 0), iota((H, L), 1)
    spread = ones((head == core * HC + (lane >> 3)) & (lane < LAN)).astype(kind)
    row, lane = iota((S * BD, L), 0), iota((S * BD, L), 1)
    total = 0.0
    for value, place in ((own, core), (other, 1 - core)):
        wide = dot(value.reshape(S * BD, H).astype(kind), spread, exact=exact)
        wide = jnp.where((row & 7) == (lane & 7), wide, 0.0)
        to, col = iota((BLK, S * BD), 0), iota((BLK, S * BD), 1)
        gather = ones((col >> 3) == to - S * place).astype(kind)
        total = total + dot(gather, wide.astype(kind), exact=exact)
    return total


def gaps(p, rows, dim):
    dims = (rows, 128) if dim == 0 else (128, rows)
    place, lane = iota(dims, dim), iota(dims, 1 - dim)
    return ones((lane == 64 * p + 2 * (place >> 4) + (place & 15) - R) & ((place & 15) >= R))


def send_kernel(
    where_am_i, source_hbm, target_hbm, live_hbm, d_hbm, own_ref, other_ref, wide_ref, out_ref, d_ref, source, target,
    live, sems
):
    moves = ((d_hbm, d_ref), (source_hbm, source), (target_hbm, target), (live_hbm, live))
    copies = [pltpu.make_async_copy(a, b, sems.at[i]) for i, (a, b) in enumerate(moves)]
    for copy in copies:
        copy.start()
    field = chip_field(own_ref[...], other_ref[...], where_am_i[0], False)
    block = packed(field).reshape(BLK, 128)
    fills = [dot(block, gaps(p, 2 * L, 1)) for p in range(2)]
    buoy = where_am_i[1]
    row, col = iota((M, L), 0), iota((M, L), 1)
    half = ones((row == HALF * (buoy & 1) + col - 2 * (col >> 4)) & ((col & 15) < R))
    to, line = iota((BLK, S), 0), iota((BLK, S), 1)
    brow, blane = iota((BLK, 2 * L), 0), iota((BLK, 2 * L), 1)
    for copy in copies:
        copy.wait()
    for k in range(2):
        at = (source[k] - (buoy - 1) * BD) * BD + target[k] - buoy * BD
        at = jnp.where(live[k] == 1, jnp.clip(at, 0, EMPTY), EMPTY)
        fills[1] = jnp.where((brow == BLK - 1) & (blane == L + k), at.astype(F32), fills[1])
    own = dot(d_ref[...], half).astype(BF16)
    for p in range(2):
        extra = []
        for k in range(2):
            spare = ((to == R) & (line == 2 * p + k)) | ((to == R + 1) & (line == 4 + 2 * p + k))
            extra.append(dot(ones(spare), own))
        extra = jnp.concatenate(extra, axis=1) + fills[p]
        for j in range(CHIPS):
            rows = wide_ref[p, R * j : min(R * j + BLK, M), :]
            if j == CHIPS - 1:
                rows = jnp.concatenate([rows, jnp.zeros((BLK - R, 2 * L), F32)], axis=0)
            rows = jnp.where(brow < R, rows, 0.0) + extra
            out_ref[j, :, 2 * L * p : 2 * L * (p + 1)] = rows.astype(BF16)


def first_kernel(in_ref, out_ref):
    block = 0.0
    for p in range(2):
        part = in_ref[:, :, 512 * p : 512 * (p + 1)].reshape(ROWS, 512)
        block = block + dot(part, gaps(p, 512, 0))
    out_ref[...] = block.reshape(CHIPS, BLK, 128).astype(BF16)


def place_kernel(
    where_am_i, own_at, other_at, in_ref, other_ref, amb_ref, amb_other_ref, w_ref, a_ref, d_ref
):
    core = where_am_i[0]
    w_ref[...] = jnp.zeros_like(w_ref)
    for j in range(CHIPS):
        for p in range(2):
            w_ref[own_at[j, 0, p]] = in_ref[j, :, 512 * p : 512 * (p + 1)]
            w_ref[other_at[j, 0, p]] = other_ref[j, :, 512 * p : 512 * (p + 1)]
    a_ref[...] = chip_field(amb_ref[...], amb_other_ref[...], core, True)
    part_rows, width = 8 * BLK, 4 * 64
    to, col = iota((part_rows, width), 0), iota((part_rows, width), 1)
    line = (to & 15) - (col >> 6)
    picks = []
    for place in (core, 1 - core):
        upper = (line == S * place) & ((col & 7) == 6)
        lower = (line == S * place + 4) & ((col & 7) == 7) & ((col >> 6) < 3)
        picks.append(ones(((to >> 4) == ((col >> 3) & 7)) & (upper | lower)))
    for g in range(CHIPS // 8):
        total = 0.0
        for ref, pick in zip((in_ref, other_ref), picks):
            cells = [
                ref[8 * g : 8 * (g + 1), 8:, L * q : L * (q + 1)].reshape(64, L) for q in range(4)
            ]
            total = total + dot(pick, jnp.concatenate(cells, axis=0))
        d_ref[part_rows * g : part_rows * (g + 1), :] = total.astype(BF16)


def weighted(w_ref, group, field):
    lane = iota((BD * BLK, L), 1)
    total = jnp.zeros((BD * BLK, L), F32)
    for b in range(BD):
        part = dot(w_ref[BD * group + b], field)
        total = total + jnp.where((lane & 7) == b, part, 0.0)
    return total


def own_kernel(w_ref, own_ref, out_ref):
    out_ref[...] = weighted(w_ref, 1, unpacked(own_ref[...]))


def low_kernel(w_ref, low_ref, part_ref, out_ref):
    out_ref[...] = part_ref[...] + weighted(w_ref, 0, unpacked(low_ref[...]))


def incident_kernel(groups, w_ref, *refs):
    fields, (part_ref, a_ref, out_ref) = refs[: len(groups)], refs[len(groups) :]
    total = part_ref[...]
    for group, field in zip(groups, fields):
        total = total + weighted(w_ref, group, unpacked(field[...]))
    row, col = iota((L, L), 0), iota((L, L), 1)
    same = ones(((row >> 3) == (col >> 3)) & (row < LAN))
    high, rest = two_terms(total)
    total = dot(high, same) + dot(rest, same)
    row, lane = iota((BLK, L), 0), iota((BLK, L), 1)
    mine = a_ref[...]
    for t in range(BD):
        mine = mine + jnp.where((lane & 7) == t, total[BLK * t : BLK * (t + 1)], 0.0)
    mine = jnp.where((row < R) & (lane < LAN), mine, 0.0)
    out_ref[...] = jnp.broadcast_to(packed(mine), (CHIPS, BLK, 128))


def coeffs_kernel(where_am_i, in_ref, d_ref, d_other_ref, out_ref):
    field = unpacked(in_ref[...])
    even = (where_am_i[1] & 1) == 0
    upper, lower = field[:L].astype(F32), field[L:].astype(F32)
    first = jnp.where(even, upper, lower).astype(BF16)
    second = jnp.where(even, lower, upper).astype(BF16)
    out_ref[...] = packed(dot(d_ref[...], first) + dot(d_other_ref[...], second))


def ready_kernel(p_ref, d_ref, p_out, d_out, lanes_out):
    p_out[...] = dot(padding(), p_ref[...]).astype(BF16)
    d_out[...] = dot(d_ref[...], packing()).astype(BF16)
    row, col = iota((L, BD * 128), 0), iota((L, BD * 128), 1)
    to = (row & 7) * 128 + (row >> 3)
    for c in range(C):
        lanes_out[c] = ones((col == to + HC * c) & (row < LAN))


def outputs(blocks, p_ref, d_ref, lanes):
    field = unpacked(blocks)
    sources = dot(field, p_ref[...], dims=(0, 0))[:LAN].astype(BF16)
    high, rest = two_terms(dot(d_ref[...], field))
    return sources, dot(high, lanes) + dot(rest, lanes)


def last_own_kernel(where_am_i, in_ref, p_ref, d_ref, lanes_ref, src_ref, out_ref):
    src_ref[...], out_ref[...] = outputs(in_ref[...], p_ref, d_ref, lanes_ref[where_am_i[0]])


def last_kernel(
    where_am_i, in_ref, p_ref, d_ref, lanes_ref, own_src_ref, own_out_ref, src_ref, out_ref
):
    core = where_am_i[0]
    other, out = outputs(in_ref[...], p_ref, d_ref, lanes_ref[1 - core])
    out = out + own_out_ref[...]
    src_ref[pl.ds(pl.multiple_of(LAN * core, BLK), LAN), :] = own_src_ref[...]
    src_ref[pl.ds(pl.multiple_of(LAN * (1 - core), BLK), LAN), :] = other
    for b in range(BD):
        out_ref[:, b, :] = out[:, 128 * b : 128 * b + H]


VM = pl.BlockSpec(memory_space=pltpu.VMEM)
SM = pl.BlockSpec(memory_space=pltpu.SMEM)
HBM = pl.BlockSpec(memory_space=pltpu.HBM)


def call(kernel, scalars, arrays, shapes, name, **kwargs):
    return pl.pallas_call(
        kernel,
        out_shape=shapes,
        in_specs=[SM] * len(scalars) + [VM] * len(arrays),
        out_specs=[VM] * len(shapes) if isinstance(shapes, tuple) else VM,
        compiler_params=pltpu.CompilerParams(vmem_limit_bytes=40 << 20),
        name=name,
        **kwargs,
    )(*scalars, *arrays)


def shape(*dims, dtype=BF16):
    return jax.ShapeDtypeStruct(dims, dtype)


def exchange(blocks):
    return lax.all_to_all(blocks, PLANE, 0, 0, tiled=True)


def swapped(value):
    return lax.ppermute(value, "c", [(0, 1), (1, 0)])


def from_previous(value):
    count = lax.axis_size("x")
    return lax.ppermute(value, "x", [(i, (i + 1) % count) for i in range(count)])


def from_next(value):
    count = lax.axis_size("x")
    return lax.ppermute(value, "x", [((i + 1) % count, i) for i in range(count)])


def slot_numbers(blocks):
    return blocks[:, BLK - 1 :, 768:770].astype(I32)


def shards(
    ambient, initial_out, translation, pair_source, pair_target, pair_live, diffract, panel_rows
):
    where_am_i = jnp.stack([lax.axis_index("c"), lax.axis_index("x")]).astype(I32)
    begin = initial_out.transpose(2, 0, 1)
    waves = ambient.transpose(2, 0, 1)
    begin_other = swapped(begin)
    waves_other = swapped(waves)
    wide = lax.dot_general(
        translation, packing(), (((2,), (0,)), ((), ())), preferred_element_type=F32
    )
    wide, waves_other = lax.optimization_barrier((wide, waves_other))
    message = pl.pallas_call(
        send_kernel,
        out_shape=shape(CHIPS, BLK, 1024),
        in_specs=[SM] + [HBM] * 4 + [VM] * 3,
        out_specs=VM,
        scratch_shapes=[
            pltpu.VMEM(diffract.shape, BF16),
            pltpu.SMEM(pair_source.shape, I32),
            pltpu.SMEM(pair_source.shape, I32),
            pltpu.SMEM(pair_source.shape, I32),
            pltpu.SemaphoreType.DMA((4,)),
        ],
        compiler_params=pltpu.CompilerParams(vmem_limit_bytes=40 << 20),
        name="send",
    )(
        where_am_i,
        *[
            pltpu.with_memory_space_constraint(value, pltpu.HBM)
            for value in (pair_source, pair_target, pair_live, diffract)
        ],
        begin,
        begin_other,
        wide,
    )
    got = exchange(message)
    got, waves = lax.optimization_barrier((got, waves))
    coeffs = call(first_kernel, (), (got,), shape(CHIPS, BLK, 128), "first")
    low, high = from_previous(coeffs), from_next(coeffs)
    got_other = swapped(got)
    matrices, own_waves, half = call(
        place_kernel,
        (where_am_i, slot_numbers(got), slot_numbers(got_other)),
        (got, got_other, waves, waves_other),
        (shape(EMPTY + BD, BLK, 512), shape(BLK, L, dtype=F32), shape(ROWS, L)),
        "place",
    )
    matrices = matrices.reshape(SOURCES + 1, BD * BLK, 512)
    other_half = from_previous(half)

    for step in range(ITERS):
        if step:
            coeffs = call(
                coeffs_kernel,
                (where_am_i,),
                (got, half, other_half),
                shape(CHIPS, BLK, 128),
                "coeffs",
            )
            low, high = from_previous(coeffs), from_next(coeffs)
            coeffs, panel_rows, diffract = lax.optimization_barrier((coeffs, panel_rows, diffract))
            ready = call(
                ready_kernel,
                (),
                (panel_rows.T, diffract),
                (shape(ROWS, panel_rows.shape[0]), shape(S, ROWS), shape(C, L, BD * 128)),
                "ready",
            )
            low, ready = lax.optimization_barrier((low, ready))
        part = call(own_kernel, (), (matrices, coeffs), shape(BD * BLK, L, dtype=F32), "own")
        groups, fields = (0, 2), (low, high)
        if step:
            low_shape = shape(BD * BLK, L, dtype=F32)
            part = call(low_kernel, (), (matrices, low, part), low_shape, "low")
            groups, fields = (2,), (high,)
        message = call(
            functools.partial(incident_kernel, groups),
            (),
            (matrices, *fields, part, own_waves),
            shape(CHIPS, BLK, 128),
            "incident",
        )
        got = exchange(message)
    other = swapped(got)
    own_sources, own_outgoing = call(
        last_own_kernel,
        (where_am_i,),
        (got, *ready),
        (shape(LAN, panel_rows.shape[0]), shape(S, BD * 128, dtype=F32)),
        "last_own",
    )
    sources, outgoing = call(
        last_kernel,
        (where_am_i,),
        (other, *ready, own_sources, own_outgoing),
        (shape(H * BD, panel_rows.shape[0]), shape(S, BD, H, dtype=F32)),
        "last",
    )
    sources = sources.reshape(H, BD, panel_rows.shape[0]).transpose(1, 0, 2)
    return outgoing.transpose(1, 2, 0), sources


def solution(mesh):
    fine = Mesh(mesh.devices.reshape(mesh.shape["buoy"], Z, Y, C), ("x", "z", "y", "c"))
    dom = ("z", "y", "c")
    in_specs = (
        P("x", None, dom),
        P("x", None, dom),
        P(("x",) + dom, None, None),
        P(("x",) + dom),
        P(("x",) + dom),
        P(("x",) + dom),
        P(dom, None),
        P(dom, None),
    )
    out_specs = (P("x", None, dom), P("x", None, dom))
    return jax.shard_map(shards, mesh=fine, in_specs=in_specs, out_specs=out_specs, check_vma=False)
```

```python
import jax
import jax.numpy as jnp
from jax import lax
from jax.experimental import pallas as pl
from jax.experimental.pallas import tpu as pltpu
from jax.sharding import Mesh, PartitionSpec as P

Z, Y, C = 8, 4, 2
PLANE = ("z", "y")
CHIPS = Z * Y
F32, BF16, I32 = jnp.float32, jnp.bfloat16, jnp.int32

BD, H, S, M = 8, 36, 7, 448
HC, R, BLK, L = H // C, S * C, 16, 256
LAN = HC * BD
ROWS = CHIPS * BLK
HALF = M // C
SOURCES = 3 * BD
EMPTY = SOURCES * BD


def iota(shape, dim):
    return lax.broadcasted_iota(I32, shape, dim)


def ones(cond):
    return jnp.where(cond, 1.0, 0.0).astype(BF16)


def dot(left, right, dims=(1, 0), exact=False):
    return lax.dot_general(
        left,
        right,
        (((dims[0],), (dims[1],)), ((), ())),
        preferred_element_type=F32,
        precision=lax.Precision.HIGHEST if exact else None,
    )


def shift(rows, cols, start, to, width):
    row, col = iota((rows, cols), 0), iota((rows, cols), 1)
    return ones((row - start == col - to) & (col >= to) & (col < to + width))


def padding():
    row, col = iota((ROWS, M), 0), iota((ROWS, M), 1)
    return ones((col == row - 2 * (row >> 4)) & ((row & 15) < R))


def packing():
    row, col = iota((M, ROWS), 0), iota((M, ROWS), 1)
    return ones((row == col - 2 * (col >> 4)) & ((col & 15) < R))


def two_terms(value):
    high = value.astype(BF16)
    return high, (value - high.astype(F32)).astype(BF16)


def blocks_iota(rows):
    dims = (rows // BLK, BLK, 128)
    return iota(dims, 1), iota(dims, 2)


def packed(field):
    rows = field.shape[0]
    frow, fcol = iota((128, 128), 0), iota((128, 128), 1)
    tail = dot(field[:, 128:].astype(BF16), ones(frow == (fcol & 15))).reshape(-1, BLK, 128)
    row, lane = blocks_iota(rows)
    tail = jnp.where(((lane >> 4) == (row & 7)) & (row < R), tail, 0.0)
    low = jnp.sum(tail[:, :8], axis=1, keepdims=True)
    high = jnp.sum(tail[:, 8:], axis=1, keepdims=True)
    main = field[:, :128].reshape(-1, BLK, 128)
    return jnp.where(row < R, main, jnp.where(row == R, low, high)).astype(BF16)


def unpacked(blocks):
    blocks = blocks.astype(F32)
    row, lane = blocks_iota(ROWS)
    tail = jnp.where(row < 8, blocks[:, R : R + 1], blocks[:, R + 1 :])
    tail = jnp.where(((lane >> 4) == (row & 7)) & (row < R), tail, 0.0)
    frow, fcol = iota((128, 128), 0), iota((128, 128), 1)
    fold = ones((fcol == (frow & 15)) & (fcol < 16))
    tail = dot(tail.reshape(ROWS, 128).astype(BF16), fold)
    main = jnp.where(row < R, blocks, 0.0).reshape(ROWS, 128)
    return jnp.concatenate([main, tail], axis=1).astype(BF16)


def chip_field(own, other, core, exact):
    head, lane = iota((H, L), 0), iota((H, L), 1)
    spread = ones((head == core * HC + (lane >> 3)) & (lane < LAN))
    row, lane = iota((S * BD, L), 0), iota((S * BD, L), 1)
    to, col = iota((BLK, S * BD), 0), iota((BLK, S * BD), 1)
    total = 0.0
    for value, place in ((own, core), (other, 1 - core)):
        gather = ones((col >> 3) == to - S * place)
        value = value.reshape(S * BD, H)
        for term in two_terms(value) if exact else (value.astype(BF16),):
            wide = jnp.where((row & 7) == (lane & 7), dot(term, spread), 0.0)
            total = total + dot(gather, wide.astype(BF16))
    return total


def gaps(p, rows, dim):
    dims = (rows, 128) if dim == 0 else (128, rows)
    place, lane = iota(dims, dim), iota(dims, 1 - dim)
    return ones((lane == 64 * p + 2 * (place >> 4) + (place & 15) - R) & ((place & 15) >= R))


def send_kernel(
    where_am_i, source_hbm, target_hbm, live_hbm, d_hbm, own_ref, other_ref, wide_ref, out_ref, d_ref, source, target,
    live, sems
):
    moves = ((d_hbm, d_ref), (source_hbm, source), (target_hbm, target), (live_hbm, live))
    copies = [pltpu.make_async_copy(a, b, sems.at[i]) for i, (a, b) in enumerate(moves)]
    for copy in copies:
        copy.start()
    field = chip_field(own_ref[...], other_ref[...], where_am_i[0], False)
    block = packed(field).reshape(BLK, 128)
    fills = [dot(block, gaps(p, 2 * L, 1)) for p in range(2)]
    buoy = where_am_i[1]
    row, col = iota((M, L), 0), iota((M, L), 1)
    half = ones((row == HALF * (buoy & 1) + col - 2 * (col >> 4)) & ((col & 15) < R))
    to, line = iota((BLK, S), 0), iota((BLK, S), 1)
    brow, blane = iota((BLK, 2 * L), 0), iota((BLK, 2 * L), 1)
    for copy in copies:
        copy.wait()
    for k in range(2):
        at = (source[k] - (buoy - 1) * BD) * BD + target[k] - buoy * BD
        at = jnp.where(live[k] == 1, jnp.clip(at, 0, EMPTY), EMPTY)
        fills[1] = jnp.where((brow == BLK - 1) & (blane == L + k), at.astype(F32), fills[1])
    own = dot(d_ref[...], half).astype(BF16)
    for p in range(2):
        extra = []
        for k in range(2):
            spare = ((to == R) & (line == 2 * p + k)) | ((to == R + 1) & (line == 4 + 2 * p + k))
            extra.append(dot(ones(spare), own))
        extra = jnp.concatenate(extra, axis=1) + fills[p]
        for j in range(CHIPS):
            rows = wide_ref[p, R * j : min(R * j + BLK, M), :]
            if j == CHIPS - 1:
                rows = jnp.concatenate([rows, jnp.zeros((BLK - R, 2 * L), F32)], axis=0)
            rows = jnp.where(brow < R, rows, 0.0) + extra
            out_ref[j, :, 2 * L * p : 2 * L * (p + 1)] = rows.astype(BF16)


def first_kernel(in_ref, out_ref):
    block = 0.0
    for p in range(2):
        part = in_ref[:, :, 512 * p : 512 * (p + 1)].reshape(ROWS, 512)
        block = block + dot(part, gaps(p, 512, 0))
    out_ref[...] = block.reshape(CHIPS, BLK, 128).astype(BF16)


def place_kernel(
    where_am_i, own_at, other_at, in_ref, other_ref, amb_ref, amb_other_ref, w_ref, a_ref, d_ref
):
    core = where_am_i[0]
    w_ref[...] = jnp.zeros_like(w_ref)
    for j in range(CHIPS):
        for p in range(2):
            w_ref[own_at[j, 0, p]] = in_ref[j, :, 512 * p : 512 * (p + 1)]
            w_ref[other_at[j, 0, p]] = other_ref[j, :, 512 * p : 512 * (p + 1)]
    a_ref[...] = chip_field(amb_ref[...], amb_other_ref[...], core, True)
    part_rows, width = 8 * BLK, 4 * 64
    to, col = iota((part_rows, width), 0), iota((part_rows, width), 1)
    line = (to & 15) - (col >> 6)
    picks = []
    for place in (core, 1 - core):
        upper = (line == S * place) & ((col & 7) == 6)
        lower = (line == S * place + 4) & ((col & 7) == 7) & ((col >> 6) < 3)
        picks.append(ones(((to >> 4) == ((col >> 3) & 7)) & (upper | lower)))
    for g in range(CHIPS // 8):
        total = 0.0
        for ref, pick in zip((in_ref, other_ref), picks):
            cells = [
                ref[8 * g : 8 * (g + 1), 8:, L * q : L * (q + 1)].reshape(64, L) for q in range(4)
            ]
            total = total + dot(pick, jnp.concatenate(cells, axis=0))
        d_ref[part_rows * g : part_rows * (g + 1), :] = total.astype(BF16)


def weighted(w_ref, group, field):
    lane = iota((BD * BLK, L), 1)
    total = jnp.zeros((BD * BLK, L), F32)
    for b in range(BD):
        part = dot(w_ref[BD * group + b], field)
        total = total + jnp.where((lane & 7) == b, part, 0.0)
    return total


def coeffs(field, d_ref):
    return (dot(d_ref[0], field[:L]) + dot(d_ref[1], field[L:])).astype(BF16)


def own_kernel(w_ref, own_ref, d_ref, out_ref):
    out_ref[...] = weighted(w_ref, 1, coeffs(unpacked(own_ref[...]), d_ref))


def low_kernel(w_ref, low_ref, d_ref, part_ref, out_ref):
    out_ref[...] = part_ref[...] + weighted(w_ref, 0, coeffs(unpacked(low_ref[...]), d_ref))


def part_kernel(w_ref, own_ref, out_ref):
    out_ref[...] = weighted(w_ref, 1, unpacked(own_ref[...]))


def first_incident_kernel(w_ref, low_ref, high_ref, part_ref, a_ref, out_ref):
    total = part_ref[...] + weighted(w_ref, 0, unpacked(low_ref[...]))
    finish(total + weighted(w_ref, 2, unpacked(high_ref[...])), a_ref, out_ref)


def last_incident_kernel(w_ref, high_ref, d_ref, part_ref, a_ref, out_ref):
    total = part_ref[...] + weighted(w_ref, 2, coeffs(unpacked(high_ref[...]), d_ref))
    finish(total, a_ref, out_ref)


def finish(total, a_ref, out_ref):
    row, col = iota((L, L), 0), iota((L, L), 1)
    same = ones(((row >> 3) == (col >> 3)) & (row < LAN))
    high, rest = two_terms(total)
    total = dot(high, same) + dot(rest, same)
    row, lane = iota((BLK, L), 0), iota((BLK, L), 1)
    mine = a_ref[...]
    for t in range(BD):
        mine = mine + jnp.where((lane & 7) == t, total[BLK * t : BLK * (t + 1)], 0.0)
    mine = jnp.where((row < R) & (lane < LAN), mine, 0.0)
    out_ref[...] = jnp.broadcast_to(packed(mine), (CHIPS, BLK, 128))


def ready_kernel(where_am_i, half_ref, other_ref, p_ref, d_ref, full_out, p_out, d_out, lanes_out):
    place = where_am_i[1] & 1
    full_out[place] = half_ref[...]
    full_out[1 - place] = other_ref[...]
    p_out[...] = dot(padding(), p_ref[...]).astype(BF16)
    d_out[...] = dot(d_ref[...], packing()).astype(BF16)
    row, col = iota((L, BD * 128), 0), iota((L, BD * 128), 1)
    to = (row & 7) * 128 + (row >> 3)
    for c in range(C):
        lanes_out[c] = ones((col == to + HC * c) & (row < LAN))


def outputs(blocks, p_ref, d_ref, lanes):
    field = unpacked(blocks)
    sources = dot(field, p_ref[...], dims=(0, 0))[:LAN].astype(BF16)
    high, rest = two_terms(dot(d_ref[...], field))
    return sources, dot(high, lanes) + dot(rest, lanes)


def last_own_kernel(where_am_i, in_ref, p_ref, d_ref, lanes_ref, src_ref, out_ref):
    src_ref[...], out_ref[...] = outputs(in_ref[...], p_ref, d_ref, lanes_ref[where_am_i[0]])


def last_kernel(
    where_am_i, in_ref, p_ref, d_ref, lanes_ref, own_src_ref, own_out_ref, src_ref, out_ref
):
    core = where_am_i[0]
    other, out = outputs(in_ref[...], p_ref, d_ref, lanes_ref[1 - core])
    out = out + own_out_ref[...]
    src_ref[pl.ds(pl.multiple_of(LAN * core, BLK), LAN), :] = own_src_ref[...]
    src_ref[pl.ds(pl.multiple_of(LAN * (1 - core), BLK), LAN), :] = other
    for b in range(BD):
        out_ref[:, b, :] = out[:, 128 * b : 128 * b + H]


VM = pl.BlockSpec(memory_space=pltpu.VMEM)
SM = pl.BlockSpec(memory_space=pltpu.SMEM)
HBM = pl.BlockSpec(memory_space=pltpu.HBM)


def call(kernel, scalars, arrays, shapes, name, **kwargs):
    return pl.pallas_call(
        kernel,
        out_shape=shapes,
        in_specs=[SM] * len(scalars) + [VM] * len(arrays),
        out_specs=[VM] * len(shapes) if isinstance(shapes, tuple) else VM,
        compiler_params=pltpu.CompilerParams(vmem_limit_bytes=40 << 20),
        name=name,
        **kwargs,
    )(*scalars, *arrays)


def shape(*dims, dtype=BF16):
    return jax.ShapeDtypeStruct(dims, dtype)


def exchange(blocks):
    return lax.all_to_all(blocks, PLANE, 0, 0, tiled=True)


def swapped(value):
    return lax.ppermute(value, "c", [(0, 1), (1, 0)])


def from_previous(value):
    count = lax.axis_size("x")
    return lax.ppermute(value, "x", [(i, (i + 1) % count) for i in range(count)])


def from_next(value):
    count = lax.axis_size("x")
    return lax.ppermute(value, "x", [((i + 1) % count, i) for i in range(count)])


def slot_numbers(blocks):
    return blocks[:, BLK - 1 :, 768:770].astype(I32)


def shards(
    ambient, initial_out, translation, pair_source, pair_target, pair_live, diffract, panel_rows
):
    where_am_i = jnp.stack([lax.axis_index("c"), lax.axis_index("x")]).astype(I32)
    begin = initial_out.transpose(2, 0, 1)
    waves = ambient.transpose(2, 0, 1)
    begin_other = swapped(begin)
    waves_other = swapped(waves)
    wide = lax.dot_general(
        translation, packing(), (((2,), (0,)), ((), ())), preferred_element_type=F32
    )
    wide, waves_other = lax.optimization_barrier((wide, waves_other))
    message = pl.pallas_call(
        send_kernel,
        out_shape=shape(CHIPS, BLK, 1024),
        in_specs=[SM] + [HBM] * 4 + [VM] * 3,
        out_specs=VM,
        scratch_shapes=[
            pltpu.VMEM(diffract.shape, BF16),
            pltpu.SMEM(pair_source.shape, I32),
            pltpu.SMEM(pair_source.shape, I32),
            pltpu.SMEM(pair_source.shape, I32),
            pltpu.SemaphoreType.DMA((4,)),
        ],
        compiler_params=pltpu.CompilerParams(vmem_limit_bytes=40 << 20),
        name="send",
    )(
        where_am_i,
        *[
            pltpu.with_memory_space_constraint(value, pltpu.HBM)
            for value in (pair_source, pair_target, pair_live, diffract)
        ],
        begin,
        begin_other,
        wide,
    )
    got = exchange(message)
    got, waves = lax.optimization_barrier((got, waves))
    first = call(first_kernel, (), (got,), shape(CHIPS, BLK, 128), "first")
    low, high = from_previous(first), from_next(first)
    got_other = swapped(got)
    matrices, own_waves, half = call(
        place_kernel,
        (where_am_i, slot_numbers(got), slot_numbers(got_other)),
        (got, got_other, waves, waves_other),
        (shape(EMPTY + BD, BLK, 512), shape(BLK, L, dtype=F32), shape(ROWS, L)),
        "place",
    )
    matrices = matrices.reshape(SOURCES + 1, BD * BLK, 512)
    other_half = from_previous(half)

    part_shape = shape(BD * BLK, L, dtype=F32)
    part = call(part_kernel, (), (matrices, first), part_shape, "part")
    got = exchange(
        call(
            first_incident_kernel,
            (),
            (matrices, low, high, part, own_waves),
            shape(CHIPS, BLK, 128),
            "incident_first",
        )
    )
    got, other_half = lax.optimization_barrier((got, other_half))
    low, high = from_previous(got), from_next(got)
    got, half, panel_rows, diffract = lax.optimization_barrier((got, half, panel_rows, diffract))
    full, *ready = call(
        ready_kernel,
        (where_am_i,),
        (half, other_half, panel_rows.T, diffract),
        (
            shape(2, ROWS, L),
            shape(ROWS, panel_rows.shape[0]),
            shape(S, ROWS),
            shape(C, L, BD * 128),
        ),
        "ready",
    )
    part = call(own_kernel, (), (matrices, got, full), part_shape, "own")
    low, part = lax.optimization_barrier((low, part))
    part = call(low_kernel, (), (matrices, low, full, part), part_shape, "low")
    got = exchange(
        call(
            last_incident_kernel,
            (),
            (matrices, high, full, part, own_waves),
            shape(CHIPS, BLK, 128),
            "incident_last",
        )
    )
    other = swapped(got)
    own_sources, own_outgoing = call(
        last_own_kernel,
        (where_am_i,),
        (got, *ready),
        (shape(LAN, panel_rows.shape[0]), shape(S, BD * 128, dtype=F32)),
        "last_own",
    )
    sources, outgoing = call(
        last_kernel,
        (where_am_i,),
        (other, *ready, own_sources, own_outgoing),
        (shape(H * BD, panel_rows.shape[0]), shape(S, BD, H, dtype=F32)),
        "last",
    )
    sources = sources.reshape(H, BD, panel_rows.shape[0]).transpose(1, 0, 2)
    return outgoing.transpose(1, 2, 0), sources


def solution(mesh):
    fine = Mesh(mesh.devices.reshape(mesh.shape["buoy"], Z, Y, C), ("x", "z", "y", "c"))
    dom = ("z", "y", "c")
    in_specs = (
        P("x", None, dom),
        P("x", None, dom),
        P(("x",) + dom, None, None),
        P(("x",) + dom),
        P(("x",) + dom),
        P(("x",) + dom),
        P(dom, None),
        P(dom, None),
    )
    out_specs = (P("x", None, dom), P("x", None, dom))
    return jax.shard_map(shards, mesh=fine, in_specs=in_specs, out_specs=out_specs, check_vma=False)
```

```python
import jax
import jax.numpy as jnp
from jax import lax
from jax.experimental import pallas as pl
from jax.experimental.pallas import tpu as pltpu
from jax.sharding import Mesh, PartitionSpec as P

Z, Y, C = 8, 4, 2
PLANE = ("z", "y")
CHIPS = Z * Y
F32, BF16, I32 = jnp.float32, jnp.bfloat16, jnp.int32

BD, H, S, M = 8, 36, 7, 448
HC, R, BLK, L = H // C, S * C, 16, 256
LAN = HC * BD
ROWS = CHIPS * BLK
HALF = M // C
SOURCES = 3 * BD
EMPTY = SOURCES * BD


def iota(shape, dim):
    return lax.broadcasted_iota(I32, shape, dim)


def ones(cond):
    return jnp.where(cond, 1.0, 0.0).astype(BF16)


def dot(left, right, dims=(1, 0), exact=False):
    return lax.dot_general(
        left,
        right,
        (((dims[0],), (dims[1],)), ((), ())),
        preferred_element_type=F32,
        precision=lax.Precision.HIGHEST if exact else None,
    )


def shift(rows, cols, start, to, width):
    row, col = iota((rows, cols), 0), iota((rows, cols), 1)
    return ones((row - start == col - to) & (col >= to) & (col < to + width))


def padding():
    row, col = iota((ROWS, M), 0), iota((ROWS, M), 1)
    return ones((col == row - 2 * (row >> 4)) & ((row & 15) < R))


def packing():
    row, col = iota((M, ROWS), 0), iota((M, ROWS), 1)
    return ones((row == col - 2 * (col >> 4)) & ((col & 15) < R))


def two_terms(value):
    high = value.astype(BF16)
    return high, (value - high.astype(F32)).astype(BF16)


def blocks_iota(rows):
    dims = (rows // BLK, BLK, 128)
    return iota(dims, 1), iota(dims, 2)


def packed(field):
    rows = field.shape[0]
    frow, fcol = iota((128, 128), 0), iota((128, 128), 1)
    tail = dot(field[:, 128:].astype(BF16), ones(frow == (fcol & 15))).reshape(-1, BLK, 128)
    row, lane = blocks_iota(rows)
    tail = jnp.where(((lane >> 4) == (row & 7)) & (row < R), tail, 0.0)
    low = jnp.sum(tail[:, :8], axis=1, keepdims=True)
    high = jnp.sum(tail[:, 8:], axis=1, keepdims=True)
    main = field[:, :128].reshape(-1, BLK, 128)
    return jnp.where(row < R, main, jnp.where(row == R, low, high)).astype(BF16)


def unpacked(blocks):
    blocks = blocks.astype(F32)
    row, lane = blocks_iota(ROWS)
    tail = jnp.where(row < 8, blocks[:, R : R + 1], blocks[:, R + 1 :])
    tail = jnp.where(((lane >> 4) == (row & 7)) & (row < R), tail, 0.0)
    frow, fcol = iota((128, 128), 0), iota((128, 128), 1)
    fold = ones((fcol == (frow & 15)) & (fcol < 16))
    tail = dot(tail.reshape(ROWS, 128).astype(BF16), fold)
    main = jnp.where(row < R, blocks, 0.0).reshape(ROWS, 128)
    return jnp.concatenate([main, tail], axis=1).astype(BF16)


def chip_field(own, other, core, exact):
    head, lane = iota((H, L), 0), iota((H, L), 1)
    spread = ones((head == core * HC + (lane >> 3)) & (lane < LAN))
    row, lane = iota((S * BD, L), 0), iota((S * BD, L), 1)
    to, col = iota((BLK, S * BD), 0), iota((BLK, S * BD), 1)
    total = 0.0
    for value, place in ((own, core), (other, 1 - core)):
        gather = ones((col >> 3) == to - S * place)
        value = value.reshape(S * BD, H)
        for term in two_terms(value) if exact else (value.astype(BF16),):
            wide = jnp.where((row & 7) == (lane & 7), dot(term, spread), 0.0)
            total = total + dot(gather, wide.astype(BF16))
    return total


def gaps(p, dim):
    place, lane = iota((128, 128), dim), iota((128, 128), 1 - dim)
    start = jnp.where((place & 15) >= R, lane - 2 * (place >> 4) - (place & 15) + R, -1)
    return jnp.concatenate([ones(start == 64 * p + 16 * t) for t in range(4)], axis=dim)


def send_kernel(
    where_am_i, source_hbm, target_hbm, live_hbm, d_hbm, own_ref, other_ref, wide_ref, out_ref, d_ref, source, target,
    live, sems
):
    moves = ((d_hbm, d_ref), (source_hbm, source), (target_hbm, target), (live_hbm, live))
    copies = [pltpu.make_async_copy(a, b, sems.at[i]) for i, (a, b) in enumerate(moves)]
    for copy in copies:
        copy.start()
    field = chip_field(own_ref[...], other_ref[...], where_am_i[0], False)
    block = packed(field).reshape(BLK, 128)
    fills = [dot(block, gaps(p, 1)) for p in range(2)]
    buoy = where_am_i[1]
    row, col = iota((M, L), 0), iota((M, L), 1)
    half = ones((row == HALF * (buoy & 1) + col - 2 * (col >> 4)) & ((col & 15) < R))
    to, line = iota((BLK, S), 0), iota((BLK, S), 1)
    brow, blane = iota((BLK, 2 * L), 0), iota((BLK, 2 * L), 1)
    for copy in copies:
        copy.wait()
    for k in range(2):
        at = (source[k] - (buoy - 1) * BD) * BD + target[k] - buoy * BD
        at = jnp.where(live[k] == 1, jnp.clip(at, 0, EMPTY), EMPTY)
        fills[1] = jnp.where((brow == BLK - 1) & (blane == L + k), at.astype(F32), fills[1])
    own = dot(d_ref[...], half).astype(BF16)
    for p in range(2):
        extra = []
        for k in range(2):
            spare = ((to == R) & (line == 2 * p + k)) | ((to == R + 1) & (line == 4 + 2 * p + k))
            extra.append(dot(ones(spare), own))
        extra = jnp.concatenate(extra, axis=1) + fills[p]
        for j in range(CHIPS):
            rows = wide_ref[p, R * j : min(R * j + BLK, M), :]
            if j == CHIPS - 1:
                rows = jnp.concatenate([rows, jnp.zeros((BLK - R, 2 * L), F32)], axis=0)
            rows = jnp.where(brow < R, rows, 0.0) + extra
            out_ref[j, :, 2 * L * p : 2 * L * (p + 1)] = rows.astype(BF16)


def first_kernel(in_ref, out_ref):
    block = 0.0
    for p in range(2):
        part = in_ref[:, :, 512 * p : 512 * (p + 1)].reshape(ROWS, 512)
        block = block + dot(part, gaps(p, 0))
    out_ref[...] = block.reshape(CHIPS, BLK, 128).astype(BF16)


def place_kernel(
    where_am_i, own_at, other_at, in_ref, other_ref, amb_ref, amb_other_ref, w_ref, a_ref, d_ref
):
    core = where_am_i[0]
    w_ref[...] = jnp.zeros_like(w_ref)
    for j in range(CHIPS):
        for p in range(2):
            w_ref[own_at[j, 0, p]] = in_ref[j, :, 512 * p : 512 * (p + 1)]
            w_ref[other_at[j, 0, p]] = other_ref[j, :, 512 * p : 512 * (p + 1)]
    a_ref[...] = chip_field(amb_ref[...], amb_other_ref[...], core, True)
    part_rows, width = 8 * BLK, 4 * 64
    to, col = iota((part_rows, width), 0), iota((part_rows, width), 1)
    line = (to & 15) - (col >> 6)
    picks = []
    for place in (core, 1 - core):
        upper = (line == S * place) & ((col & 7) == 6)
        lower = (line == S * place + 4) & ((col & 7) == 7) & ((col >> 6) < 3)
        picks.append(ones(((to >> 4) == ((col >> 3) & 7)) & (upper | lower)))
    for g in range(CHIPS // 8):
        total = 0.0
        for ref, pick in zip((in_ref, other_ref), picks):
            cells = [
                ref[8 * g : 8 * (g + 1), 8:, L * q : L * (q + 1)].reshape(64, L) for q in range(4)
            ]
            total = total + dot(pick, jnp.concatenate(cells, axis=0))
        d_ref[part_rows * g : part_rows * (g + 1), :] = total.astype(BF16)


def weighted(w_ref, group, field):
    lane = iota((BD * BLK, L), 1)
    total = jnp.zeros((BD * BLK, L), F32)
    for b in range(BD):
        part = dot(w_ref[BD * group + b], field)
        total = total + jnp.where((lane & 7) == b, part, 0.0)
    return total


def coeffs(field, d_ref):
    return dot(d_ref[...], field).astype(BF16)


def own_kernel(w_ref, own_ref, d_ref, out_ref):
    out_ref[...] = weighted(w_ref, 1, coeffs(unpacked(own_ref[...]), d_ref))


def low_kernel(w_ref, low_ref, d_ref, part_ref, out_ref):
    out_ref[...] = part_ref[...] + weighted(w_ref, 0, coeffs(unpacked(low_ref[...]), d_ref))


def part_kernel(w_ref, own_ref, out_ref):
    out_ref[...] = weighted(w_ref, 1, unpacked(own_ref[...]))


def first_incident_kernel(w_ref, low_ref, high_ref, part_ref, a_ref, out_ref):
    total = part_ref[...] + weighted(w_ref, 0, unpacked(low_ref[...]))
    finish(total + weighted(w_ref, 2, unpacked(high_ref[...])), a_ref, out_ref)


def last_incident_kernel(w_ref, high_ref, d_ref, part_ref, a_ref, out_ref):
    total = part_ref[...] + weighted(w_ref, 2, coeffs(unpacked(high_ref[...]), d_ref))
    finish(total, a_ref, out_ref)


def finish(total, a_ref, out_ref):
    row, col = iota((L, L), 0), iota((L, L), 1)
    same = ones(((row >> 3) == (col >> 3)) & (row < LAN))
    high, rest = two_terms(total)
    total = dot(high, same) + dot(rest, same)
    row, lane = iota((BLK, L), 0), iota((BLK, L), 1)
    mine = a_ref[...]
    for t in range(BD):
        mine = mine + jnp.where((lane & 7) == t, total[BLK * t : BLK * (t + 1)], 0.0)
    mine = jnp.where((row < R) & (lane < LAN), mine, 0.0)
    out_ref[...] = jnp.broadcast_to(packed(mine), (CHIPS, BLK, 128))


def ready_kernel(where_am_i, half_ref, other_ref, p_ref, d_ref, full_out, p_out, d_out, lanes_out):
    even = (where_am_i[1] & 1) == 0
    half, other = half_ref[...].astype(F32), other_ref[...].astype(F32)
    full_out[:, :L] = jnp.where(even, half, other).astype(BF16)
    full_out[:, L:] = jnp.where(even, other, half).astype(BF16)
    p_out[...] = dot(padding(), p_ref[...]).astype(BF16)
    d_out[...] = dot(d_ref[...], packing()).astype(BF16)
    row, col = iota((L, BD * 128), 0), iota((L, BD * 128), 1)
    to = (row & 7) * 128 + (row >> 3)
    for c in range(C):
        lanes_out[c] = ones((col == to + HC * c) & (row < LAN))


def outputs(blocks, p_ref, d_ref, lanes):
    field = unpacked(blocks)
    sources = dot(field, p_ref[...], dims=(0, 0))[:LAN].astype(BF16)
    high, rest = two_terms(dot(d_ref[...], field))
    return sources, dot(high, lanes) + dot(rest, lanes)


def last_own_kernel(where_am_i, in_ref, p_ref, d_ref, lanes_ref, src_ref, out_ref):
    src_ref[...], out_ref[...] = outputs(in_ref[...], p_ref, d_ref, lanes_ref[where_am_i[0]])


def last_kernel(
    where_am_i, in_ref, p_ref, d_ref, lanes_ref, own_src_ref, own_out_ref, src_ref, out_ref
):
    core = where_am_i[0]
    other, out = outputs(in_ref[...], p_ref, d_ref, lanes_ref[1 - core])
    out = out + own_out_ref[...]
    src_ref[pl.ds(pl.multiple_of(LAN * core, BLK), LAN), :] = own_src_ref[...]
    src_ref[pl.ds(pl.multiple_of(LAN * (1 - core), BLK), LAN), :] = other
    for b in range(BD):
        out_ref[:, b, :] = out[:, 128 * b : 128 * b + H]


VM = pl.BlockSpec(memory_space=pltpu.VMEM)
SM = pl.BlockSpec(memory_space=pltpu.SMEM)
HBM = pl.BlockSpec(memory_space=pltpu.HBM)


def call(kernel, scalars, arrays, shapes, name, **kwargs):
    return pl.pallas_call(
        kernel,
        out_shape=shapes,
        in_specs=[SM] * len(scalars) + [VM] * len(arrays),
        out_specs=[VM] * len(shapes) if isinstance(shapes, tuple) else VM,
        compiler_params=pltpu.CompilerParams(vmem_limit_bytes=40 << 20),
        name=name,
        **kwargs,
    )(*scalars, *arrays)


def shape(*dims, dtype=BF16):
    return jax.ShapeDtypeStruct(dims, dtype)


def exchange(blocks):
    return lax.all_to_all(blocks, PLANE, 0, 0, tiled=True)


def swapped(value):
    return lax.ppermute(value, "c", [(0, 1), (1, 0)])


def from_previous(value):
    count = lax.axis_size("x")
    return lax.ppermute(value, "x", [(i, (i + 1) % count) for i in range(count)])


def from_next(value):
    count = lax.axis_size("x")
    return lax.ppermute(value, "x", [((i + 1) % count, i) for i in range(count)])


def slot_numbers(blocks):
    return blocks[:, BLK - 1 :, 768:770].astype(I32)


def shards(
    ambient, initial_out, translation, pair_source, pair_target, pair_live, diffract, panel_rows
):
    where_am_i = jnp.stack([lax.axis_index("c"), lax.axis_index("x")]).astype(I32)
    begin = initial_out.transpose(2, 0, 1)
    waves = ambient.transpose(2, 0, 1)
    begin_other = swapped(begin)
    waves_other = swapped(waves)
    wide = lax.dot_general(
        translation, packing(), (((2,), (0,)), ((), ())), preferred_element_type=F32
    )
    wide, waves_other = lax.optimization_barrier((wide, waves_other))
    message = pl.pallas_call(
        send_kernel,
        out_shape=shape(CHIPS, BLK, 1024),
        in_specs=[SM] + [HBM] * 4 + [VM] * 3,
        out_specs=VM,
        scratch_shapes=[
            pltpu.VMEM(diffract.shape, BF16),
            pltpu.SMEM(pair_source.shape, I32),
            pltpu.SMEM(pair_source.shape, I32),
            pltpu.SMEM(pair_source.shape, I32),
            pltpu.SemaphoreType.DMA((4,)),
        ],
        compiler_params=pltpu.CompilerParams(vmem_limit_bytes=40 << 20),
        name="send",
    )(
        where_am_i,
        *[
            pltpu.with_memory_space_constraint(value, pltpu.HBM)
            for value in (pair_source, pair_target, pair_live, diffract)
        ],
        begin,
        begin_other,
        wide,
    )
    got = exchange(message)
    got, waves = lax.optimization_barrier((got, waves))
    first = call(first_kernel, (), (got,), shape(CHIPS, BLK, 128), "first")
    low, high = from_previous(first), from_next(first)
    got_other = swapped(got)
    matrices, own_waves, half = call(
        place_kernel,
        (where_am_i, slot_numbers(got), slot_numbers(got_other)),
        (got, got_other, waves, waves_other),
        (shape(EMPTY + BD, BLK, 512), shape(BLK, L, dtype=F32), shape(ROWS, L)),
        "place",
    )
    matrices = matrices.reshape(SOURCES + 1, BD * BLK, 512)
    other_half = from_previous(half)

    part_shape = shape(BD * BLK, L, dtype=F32)
    part = call(part_kernel, (), (matrices, first), part_shape, "part")
    got = exchange(
        call(
            first_incident_kernel,
            (),
            (matrices, low, high, part, own_waves),
            shape(CHIPS, BLK, 128),
            "incident_first",
        )
    )
    got, other_half = lax.optimization_barrier((got, other_half))
    low, high = from_previous(got), from_next(got)
    got, half, panel_rows, diffract = lax.optimization_barrier((got, half, panel_rows, diffract))
    full, *ready = call(
        ready_kernel,
        (where_am_i,),
        (half, other_half, panel_rows.T, diffract),
        (
            shape(ROWS, 2 * L),
            shape(ROWS, panel_rows.shape[0]),
            shape(S, ROWS),
            shape(C, L, BD * 128),
        ),
        "ready",
    )
    part = call(own_kernel, (), (matrices, got, full), part_shape, "own")
    low, part = lax.optimization_barrier((low, part))
    part = call(low_kernel, (), (matrices, low, full, part), part_shape, "low")
    got = exchange(
        call(
            last_incident_kernel,
            (),
            (matrices, high, full, part, own_waves),
            shape(CHIPS, BLK, 128),
            "incident_last",
        )
    )
    other = swapped(got)
    own_sources, own_outgoing = call(
        last_own_kernel,
        (where_am_i,),
        (got, *ready),
        (shape(LAN, panel_rows.shape[0]), shape(S, BD * 128, dtype=F32)),
        "last_own",
    )
    sources, outgoing = call(
        last_kernel,
        (where_am_i,),
        (other, *ready, own_sources, own_outgoing),
        (shape(H * BD, panel_rows.shape[0]), shape(S, BD, H, dtype=F32)),
        "last",
    )
    sources = sources.reshape(H, BD, panel_rows.shape[0]).transpose(1, 0, 2)
    return outgoing.transpose(1, 2, 0), sources


def solution(mesh):
    fine = Mesh(mesh.devices.reshape(mesh.shape["buoy"], Z, Y, C), ("x", "z", "y", "c"))
    dom = ("z", "y", "c")
    in_specs = (
        P("x", None, dom),
        P("x", None, dom),
        P(("x",) + dom, None, None),
        P(("x",) + dom),
        P(("x",) + dom),
        P(("x",) + dom),
        P(dom, None),
        P(dom, None),
    )
    out_specs = (P("x", None, dom), P("x", None, dom))
    return jax.shard_map(shards, mesh=fine, in_specs=in_specs, out_specs=out_specs, check_vma=False)
```

```python
import jax
import jax.numpy as jnp
from jax import lax
from jax.experimental import pallas as pl
from jax.experimental.pallas import tpu as pltpu
from jax.sharding import Mesh, PartitionSpec as P

Z, Y, C = 8, 4, 2
PLANE = ("z", "y")
CHIPS = Z * Y
F32, BF16, I32 = jnp.float32, jnp.bfloat16, jnp.int32

BD, H, S, M = 8, 36, 7, 448
HC, R, BLK, L = H // C, S * C, 16, 256
LAN = HC * BD
ROWS = CHIPS * BLK
HALF = M // C
SOURCES = 3 * BD
EMPTY = SOURCES * BD


def iota(shape, dim):
    return lax.broadcasted_iota(I32, shape, dim)


def ones(cond):
    return jnp.where(cond, 1.0, 0.0).astype(BF16)


def dot(left, right, dims=(1, 0), exact=False):
    return lax.dot_general(
        left,
        right,
        (((dims[0],), (dims[1],)), ((), ())),
        preferred_element_type=F32,
        precision=lax.Precision.HIGHEST if exact else None,
    )


def shift(rows, cols, start, to, width):
    row, col = iota((rows, cols), 0), iota((rows, cols), 1)
    return ones((row - start == col - to) & (col >= to) & (col < to + width))


def padding():
    row, col = iota((ROWS, M), 0), iota((ROWS, M), 1)
    return ones((col == row - 2 * (row >> 4)) & ((row & 15) < R))


def packing():
    row, col = iota((M, ROWS), 0), iota((M, ROWS), 1)
    return ones((row == col - 2 * (col >> 4)) & ((col & 15) < R))


def two_terms(value):
    high = value.astype(BF16)
    return high, (value - high.astype(F32)).astype(BF16)


def blocks_iota(rows):
    dims = (rows // BLK, BLK, 128)
    return iota(dims, 1), iota(dims, 2)


def packed(field):
    rows = field.shape[0]
    frow, fcol = iota((128, 128), 0), iota((128, 128), 1)
    tail = dot(field[:, 128:].astype(BF16), ones(frow == (fcol & 15))).reshape(-1, BLK, 128)
    row, lane = blocks_iota(rows)
    tail = jnp.where(((lane >> 4) == (row & 7)) & (row < R), tail, 0.0)
    low = jnp.sum(tail[:, :8], axis=1, keepdims=True)
    high = jnp.sum(tail[:, 8:], axis=1, keepdims=True)
    main = field[:, :128].reshape(-1, BLK, 128)
    return jnp.where(row < R, main, jnp.where(row == R, low, high)).astype(BF16)


def unpacked(blocks):
    blocks = blocks.astype(F32)
    row, lane = blocks_iota(ROWS)
    tail = jnp.where(row < 8, blocks[:, R : R + 1], blocks[:, R + 1 :])
    tail = jnp.where(((lane >> 4) == (row & 7)) & (row < R), tail, 0.0)
    frow, fcol = iota((128, 128), 0), iota((128, 128), 1)
    fold = ones((fcol == (frow & 15)) & (fcol < 16))
    tail = dot(tail.reshape(ROWS, 128).astype(BF16), fold)
    main = jnp.where(row < R, blocks, 0.0).reshape(ROWS, 128)
    return jnp.concatenate([main, tail], axis=1).astype(BF16)


def chip_field(own, other, core, exact):
    head, lane = iota((H, L), 0), iota((H, L), 1)
    spread = ones((head == core * HC + (lane >> 3)) & (lane < LAN))
    row, lane = iota((S * BD, L), 0), iota((S * BD, L), 1)
    to, col = iota((BLK, S * BD), 0), iota((BLK, S * BD), 1)
    total = 0.0
    for value, place in ((own, core), (other, 1 - core)):
        gather = ones((col >> 3) == to - S * place)
        value = value.reshape(S * BD, H)
        for term in two_terms(value) if exact else (value.astype(BF16),):
            wide = jnp.where((row & 7) == (lane & 7), dot(term, spread), 0.0)
            total = total + dot(gather, wide.astype(BF16))
    return total


def gaps(p, dim):
    place, lane = iota((128, 128), dim), iota((128, 128), 1 - dim)
    start = jnp.where((place & 15) >= R, lane - 2 * (place >> 4) - (place & 15) + R, -1)
    return jnp.concatenate([ones(start == 64 * p + 16 * t) for t in range(4)], axis=dim)


def send_kernel(
    where_am_i, source_hbm, target_hbm, live_hbm, d_hbm, own_ref, other_ref, wide_ref, out_ref, d_ref, source, target,
    live, sems
):
    moves = ((d_hbm, d_ref), (source_hbm, source), (target_hbm, target), (live_hbm, live))
    copies = [pltpu.make_async_copy(a, b, sems.at[i]) for i, (a, b) in enumerate(moves)]
    for copy in copies:
        copy.start()
    field = chip_field(own_ref[...], other_ref[...], where_am_i[0], False)
    block = packed(field).reshape(BLK, 128)
    fills = [dot(block, gaps(p, 1)) for p in range(2)]
    buoy = where_am_i[1]
    row, col = iota((M, L), 0), iota((M, L), 1)
    half = ones((row == HALF * (buoy & 1) + col - 2 * (col >> 4)) & ((col & 15) < R))
    to, line = iota((BLK, S), 0), iota((BLK, S), 1)
    brow, blane = iota((BLK, 2 * L), 0), iota((BLK, 2 * L), 1)
    for copy in copies:
        copy.wait()
    for k in range(2):
        at = (source[k] - (buoy - 1) * BD) * BD + target[k] - buoy * BD
        at = jnp.where(live[k] == 1, jnp.clip(at, 0, EMPTY), EMPTY)
        fills[1] = jnp.where((brow == BLK - 1) & (blane == L + k), at.astype(F32), fills[1])
    own = dot(d_ref[...], half).astype(BF16)
    for p in range(2):
        extra = []
        for k in range(2):
            spare = ((to == R) & (line == 2 * p + k)) | ((to == R + 1) & (line == 4 + 2 * p + k))
            extra.append(dot(ones(spare), own))
        extra = jnp.concatenate(extra, axis=1) + fills[p]
        for j in range(CHIPS):
            rows = wide_ref[p, R * j : min(R * j + BLK, M), :]
            if j == CHIPS - 1:
                rows = jnp.concatenate([rows, jnp.zeros((BLK - R, 2 * L), F32)], axis=0)
            rows = jnp.where(brow < R, rows, 0.0) + extra
            out_ref[j, :, 2 * L * p : 2 * L * (p + 1)] = rows.astype(BF16)


def first_kernel(in_ref, out_ref):
    block = 0.0
    for p in range(2):
        part = in_ref[:, :, 512 * p : 512 * (p + 1)].reshape(ROWS, 512)
        block = block + dot(part, gaps(p, 0))
    out_ref[...] = block.reshape(CHIPS, BLK, 128).astype(BF16)


def place_kernel(
    where_am_i, own_at, other_at, in_ref, other_ref, amb_ref, amb_other_ref, w_ref, a_ref, d_ref
):
    core = where_am_i[0]
    w_ref[...] = jnp.zeros_like(w_ref)
    for j in range(CHIPS):
        for p in range(2):
            w_ref[own_at[j, 0, p]] = in_ref[j, :, 512 * p : 512 * (p + 1)]
            w_ref[other_at[j, 0, p]] = other_ref[j, :, 512 * p : 512 * (p + 1)]
    a_ref[...] = chip_field(amb_ref[...], amb_other_ref[...], core, True)
    part_rows, width = 8 * BLK, 4 * 64
    to, col = iota((part_rows, width), 0), iota((part_rows, width), 1)
    line = (to & 15) - (col >> 6)
    picks = []
    for place in (core, 1 - core):
        upper = (line == S * place) & ((col & 7) == 6)
        lower = (line == S * place + 4) & ((col & 7) == 7) & ((col >> 6) < 3)
        picks.append(ones(((to >> 4) == ((col >> 3) & 7)) & (upper | lower)))
    for g in range(CHIPS // 8):
        total = 0.0
        for ref, pick in zip((in_ref, other_ref), picks):
            cells = [
                ref[8 * g : 8 * (g + 1), 8:, L * q : L * (q + 1)].reshape(64, L) for q in range(4)
            ]
            total = total + dot(pick, jnp.concatenate(cells, axis=0))
        d_ref[part_rows * g : part_rows * (g + 1), :] = total.astype(BF16)


def weighted(w_ref, group, field):
    lane = iota((BD * BLK, L), 1)
    total = jnp.zeros((BD * BLK, L), F32)
    for b in range(BD):
        part = dot(w_ref[BD * group + b], field)
        total = total + jnp.where((lane & 7) == b, part, 0.0)
    return total


def coeffs(field, d_ref):
    return dot(d_ref[...], field).astype(BF16)


def own_kernel(w_ref, own_ref, d_ref, out_ref):
    out_ref[...] = weighted(w_ref, 1, coeffs(unpacked(own_ref[...]), d_ref))


def low_kernel(w_ref, low_ref, d_ref, part_ref, out_ref):
    out_ref[...] = part_ref[...] + weighted(w_ref, 0, coeffs(unpacked(low_ref[...]), d_ref))


def part_kernel(w_ref, own_ref, out_ref):
    out_ref[...] = weighted(w_ref, 1, unpacked(own_ref[...]))


def first_incident_kernel(w_ref, low_ref, high_ref, part_ref, a_ref, out_ref):
    total = part_ref[...] + weighted(w_ref, 0, unpacked(low_ref[...]))
    finish(total + weighted(w_ref, 2, unpacked(high_ref[...])), a_ref, out_ref)


def last_incident_kernel(w_ref, high_ref, d_ref, part_ref, a_ref, out_ref):
    total = part_ref[...] + weighted(w_ref, 2, coeffs(unpacked(high_ref[...]), d_ref))
    finish(total, a_ref, out_ref)


def finish(total, a_ref, out_ref):
    row, col = iota((L, L), 0), iota((L, L), 1)
    same = ones(((row >> 3) == (col >> 3)) & (row < LAN))
    high, rest = two_terms(total)
    total = dot(jnp.concatenate([high, rest], axis=0), same)
    total = total[: BD * BLK] + total[BD * BLK :]
    row, lane = iota((BLK, L), 0), iota((BLK, L), 1)
    mine = a_ref[...]
    for t in range(BD):
        mine = mine + jnp.where((lane & 7) == t, total[BLK * t : BLK * (t + 1)], 0.0)
    mine = jnp.where((row < R) & (lane < LAN), mine, 0.0)
    out_ref[...] = jnp.broadcast_to(packed(mine), (CHIPS, BLK, 128))


def ready_kernel(where_am_i, half_ref, other_ref, p_ref, d_ref, full_out, p_out, d_out, lanes_out):
    even = (where_am_i[1] & 1) == 0
    half, other = half_ref[...].astype(F32), other_ref[...].astype(F32)
    full_out[:, :L] = jnp.where(even, half, other).astype(BF16)
    full_out[:, L:] = jnp.where(even, other, half).astype(BF16)
    p_out[...] = dot(padding(), p_ref[...]).astype(BF16)
    d_out[...] = dot(d_ref[...], packing()).astype(BF16)
    row, col = iota((L, BD * 128), 0), iota((L, BD * 128), 1)
    to = (row & 7) * 128 + (row >> 3)
    for c in range(C):
        lanes_out[c] = ones((col == to + HC * c) & (row < LAN))


def outputs(blocks, p_ref, d_ref, lanes):
    field = unpacked(blocks)
    sources = dot(field, p_ref[...], dims=(0, 0))[:LAN].astype(BF16)
    high, rest = two_terms(dot(d_ref[...], field))
    return sources, dot(high, lanes) + dot(rest, lanes)


def last_own_kernel(where_am_i, in_ref, p_ref, d_ref, lanes_ref, src_ref, out_ref):
    src_ref[...], out_ref[...] = outputs(in_ref[...], p_ref, d_ref, lanes_ref[where_am_i[0]])


def last_kernel(
    where_am_i, in_ref, p_ref, d_ref, lanes_ref, own_src_ref, own_out_ref, src_ref, out_ref
):
    core = where_am_i[0]
    other, out = outputs(in_ref[...], p_ref, d_ref, lanes_ref[1 - core])
    out = out + own_out_ref[...]
    src_ref[pl.ds(pl.multiple_of(LAN * core, BLK), LAN), :] = own_src_ref[...]
    src_ref[pl.ds(pl.multiple_of(LAN * (1 - core), BLK), LAN), :] = other
    for b in range(BD):
        out_ref[:, b, :] = out[:, 128 * b : 128 * b + H]


VM = pl.BlockSpec(memory_space=pltpu.VMEM)
SM = pl.BlockSpec(memory_space=pltpu.SMEM)
HBM = pl.BlockSpec(memory_space=pltpu.HBM)


def call(kernel, scalars, arrays, shapes, name, **kwargs):
    return pl.pallas_call(
        kernel,
        out_shape=shapes,
        in_specs=[SM] * len(scalars) + [VM] * len(arrays),
        out_specs=[VM] * len(shapes) if isinstance(shapes, tuple) else VM,
        compiler_params=pltpu.CompilerParams(vmem_limit_bytes=40 << 20),
        name=name,
        **kwargs,
    )(*scalars, *arrays)


def shape(*dims, dtype=BF16):
    return jax.ShapeDtypeStruct(dims, dtype)


def exchange(blocks):
    return lax.all_to_all(blocks, PLANE, 0, 0, tiled=True)


def swapped(value):
    return lax.ppermute(value, "c", [(0, 1), (1, 0)])


def from_previous(value):
    count = lax.axis_size("x")
    return lax.ppermute(value, "x", [(i, (i + 1) % count) for i in range(count)])


def from_next(value):
    count = lax.axis_size("x")
    return lax.ppermute(value, "x", [((i + 1) % count, i) for i in range(count)])


def slot_numbers(blocks):
    return blocks[:, BLK - 1 :, 768:770].astype(I32)


def shards(
    ambient, initial_out, translation, pair_source, pair_target, pair_live, diffract, panel_rows
):
    where_am_i = jnp.stack([lax.axis_index("c"), lax.axis_index("x")]).astype(I32)
    begin = initial_out.transpose(2, 0, 1)
    waves = ambient.transpose(2, 0, 1)
    begin_other = swapped(begin)
    waves_other = swapped(waves)
    wide = lax.dot_general(
        translation, packing(), (((2,), (0,)), ((), ())), preferred_element_type=F32
    )
    wide, waves_other = lax.optimization_barrier((wide, waves_other))
    message = pl.pallas_call(
        send_kernel,
        out_shape=shape(CHIPS, BLK, 1024),
        in_specs=[SM] + [HBM] * 4 + [VM] * 3,
        out_specs=VM,
        scratch_shapes=[
            pltpu.VMEM(diffract.shape, BF16),
            pltpu.SMEM(pair_source.shape, I32),
            pltpu.SMEM(pair_source.shape, I32),
            pltpu.SMEM(pair_source.shape, I32),
            pltpu.SemaphoreType.DMA((4,)),
        ],
        compiler_params=pltpu.CompilerParams(vmem_limit_bytes=40 << 20),
        name="send",
    )(
        where_am_i,
        *[
            pltpu.with_memory_space_constraint(value, pltpu.HBM)
            for value in (pair_source, pair_target, pair_live, diffract)
        ],
        begin,
        begin_other,
        wide,
    )
    got = exchange(message)
    got, waves = lax.optimization_barrier((got, waves))
    first = call(first_kernel, (), (got,), shape(CHIPS, BLK, 128), "first")
    low, high = from_previous(first), from_next(first)
    got_other = swapped(got)
    matrices, own_waves, half = call(
        place_kernel,
        (where_am_i, slot_numbers(got), slot_numbers(got_other)),
        (got, got_other, waves, waves_other),
        (shape(EMPTY + BD, BLK, 512), shape(BLK, L, dtype=F32), shape(ROWS, L)),
        "place",
    )
    matrices = matrices.reshape(SOURCES + 1, BD * BLK, 512)
    other_half = from_previous(half)

    part_shape = shape(BD * BLK, L, dtype=F32)
    part = call(part_kernel, (), (matrices, first), part_shape, "part")
    got = exchange(
        call(
            first_incident_kernel,
            (),
            (matrices, low, high, part, own_waves),
            shape(CHIPS, BLK, 128),
            "incident_first",
        )
    )
    got, other_half = lax.optimization_barrier((got, other_half))
    low, high = from_previous(got), from_next(got)
    got, half, panel_rows, diffract = lax.optimization_barrier((got, half, panel_rows, diffract))
    full, *ready = call(
        ready_kernel,
        (where_am_i,),
        (half, other_half, panel_rows.T, diffract),
        (
            shape(ROWS, 2 * L),
            shape(ROWS, panel_rows.shape[0]),
            shape(S, ROWS),
            shape(C, L, BD * 128),
        ),
        "ready",
    )
    part = call(own_kernel, (), (matrices, got, full), part_shape, "own")
    low, part = lax.optimization_barrier((low, part))
    part = call(low_kernel, (), (matrices, low, full, part), part_shape, "low")
    got = exchange(
        call(
            last_incident_kernel,
            (),
            (matrices, high, full, part, own_waves),
            shape(CHIPS, BLK, 128),
            "incident_last",
        )
    )
    other = swapped(got)
    own_sources, own_outgoing = call(
        last_own_kernel,
        (where_am_i,),
        (got, *ready),
        (shape(LAN, panel_rows.shape[0]), shape(S, BD * 128, dtype=F32)),
        "last_own",
    )
    sources, outgoing = call(
        last_kernel,
        (where_am_i,),
        (other, *ready, own_sources, own_outgoing),
        (shape(H * BD, panel_rows.shape[0]), shape(S, BD, H, dtype=F32)),
        "last",
    )
    sources = sources.reshape(H, BD, panel_rows.shape[0]).transpose(1, 0, 2)
    return outgoing.transpose(1, 2, 0), sources


def solution(mesh):
    fine = Mesh(mesh.devices.reshape(mesh.shape["buoy"], Z, Y, C), ("x", "z", "y", "c"))
    dom = ("z", "y", "c")
    in_specs = (
        P("x", None, dom),
        P("x", None, dom),
        P(("x",) + dom, None, None),
        P(("x",) + dom),
        P(("x",) + dom),
        P(("x",) + dom),
        P(dom, None),
        P(dom, None),
    )
    out_specs = (P("x", None, dom), P("x", None, dom))
    return jax.shard_map(shards, mesh=fine, in_specs=in_specs, out_specs=out_specs, check_vma=False)
```
